128 devices in a mesh: inst: 32 (over x, y, core), arch: 4 (over z).
Axes of the slice: x: 4, y: 4, z: 4, core: 2. Of those that a mesh axis runs over, the one named last changes fastest.
Arguments:
- instance_arch: int32 [8192], P(('inst', 'arch')), may hold values from 0 to 39
- instance_param: int32 [8192], P(('inst', 'arch')), may hold values from 0 to 1023
- instance_ports: int32 [8192, 4], P(('inst', 'arch')), may hold values from 0 to 16383, as said below
- port_row: int32 [16384], replicated, may hold values from 0 to 16383, as said below
- param_table: float32 [1024, 64], replicated, may hold values from 0.5 to 2
- bubble_inverse: float32 [40, 64, 64], P('arch'), as said below
- coupling: float32 [40, 64, 128], P('arch'), may hold values from -0.75 to 0.75
- port_stiffness: float32 [40, 128, 128], P('arch'), as said below
- coupling_offset: float32 [8192, 64, 128], P(('inst', 'arch')), may hold values from -0.375 to 0.375
Outputs:
- assembled: float32 [16384, 7168], P(('inst', 'arch'))
The draws below stay inside these ranges and needn't reach their ends.
Inputs may be any that keep to these rules, and one draw needn't show every extreme that they name: `instance_ports`: every port is named exactly twice: once at slot 0 and once at slot 1 of two different instances, or once at slot 2 and once at slot 3 of two different instances; an instance's four ports are distinct. `port_row`: A permutation of the ports. Among the 256 port slots of one device's instances, at most 3 name ports whose row lies in one device's (128) rows, and this many is reached. `bubble_inverse`: each matrix is symmetric. `port_stiffness`: each matrix is symmetric.
All inputs are finite; a program needn't handle non-finite values.
Results may differ from the reference program's by a relative error of at most 0.00013.
Values sent between devices are 32-bit elements; how exact they have to be, the bound alone decides.
A program may use at most 128 MiB of HBM per device.

```python
import math
import jax
import jax.numpy as jnp
import numpy as np
from jax import lax

M = 64
P_SIZE = 32
NARCH = 40
NPARAM = 1024
INST_DEV = 64
NINST = 8192
NPORTS = 16384
N_INST = 32
N_ARCH = 4


def port_layout(key):
    owners = N_INST * N_ARCH
    groups = owners // 4
    base = 4 * INST_DEV // owners
    spare = base // 2
    key_offsets = jax.random.fold_in(key, 1)
    key_counts = jax.random.fold_in(key, 2)
    key_local = jax.random.fold_in(key, 3)
    key_target = jax.random.fold_in(key, 4)
    key_rows = jax.random.fold_in(key, 5)
    offsets = jax.random.permutation(key_offsets, owners).reshape(4, groups)
    surplus = jax.random.randint(key_counts, (4, groups // 2), 0, spare + 1)
    surplus = surplus.at[:, 0].set(spare)
    counts = jnp.concatenate([base + surplus, base - surplus], axis=1)
    ends = jnp.cumsum(counts, axis=1)
    positions = jnp.arange(INST_DEV)
    group_ids = jnp.sum((ends[:, None, :] <= positions[None, :, None]).astype(jnp.int32), axis=2)
    offset_of = jnp.take_along_axis(offsets, group_ids, axis=1)
    local_keys = jax.random.split(key_local, 4 * owners)
    position = jax.vmap(lambda subkey: jax.random.permutation(subkey, INST_DEV))(local_keys).reshape(4, owners, INST_DEV)
    target_keys = jax.random.split(key_target, 4 * owners)
    ordinal_map = jax.vmap(lambda subkey: jax.random.permutation(subkey, INST_DEV))(target_keys).reshape(4 * owners * INST_DEV)
    offset_at = jnp.take_along_axis(jnp.broadcast_to(offset_of[:, None, :], (4, owners, INST_DEV)), position, axis=2)
    source = jnp.arange(owners)[None, :, None]
    slot_ids = jnp.arange(4)[:, None, None]
    owner_ids = (source + offset_at) % owners
    flat_index = (slot_ids * owners + owner_ids) * INST_DEV + position
    ordinal = ordinal_map[flat_index]
    row_ids = owner_ids * (2 * INST_DEV) + slot_ids // 2 * INST_DEV + ordinal
    port_row = jax.random.permutation(key_rows, NPORTS)
    inverse = jnp.argsort(port_row)
    port_ids = inverse[row_ids]
    port_ids = jnp.transpose(port_ids, (1, 2, 0)).reshape(NINST, 4)
    return (port_ids.astype(jnp.int32), port_row.astype(jnp.int32))


def symmetric(key, size, lower, upper, spread):
    key_noise = jax.random.fold_in(key, 21)
    key_diag = jax.random.fold_in(key, 22)
    noise = jax.random.uniform(key_noise, (NARCH, size, size), jnp.float32, -1.0, 1.0)
    noise = 0.5 * (noise + jnp.swapaxes(noise, 1, 2))
    diagonal = jnp.exp(jax.random.uniform(key_diag, (NARCH, size), jnp.float32, math.log(lower), math.log(upper)))
    identity = jnp.eye(size, dtype=jnp.float32)
    return noise * (1.0 - identity) * (spread / size) + identity * diagonal[:, :, None]


def draw_instance_ports(key, part):
    port_ids, port_row = port_layout(jax.random.fold_in(key, 11))
    return port_ids


def draw_port_row(key, part):
    port_ids, port_row = port_layout(jax.random.fold_in(key, 11))
    return port_row


def draw_bubble_inverse(key, part):
    return symmetric(key, M, 3.0, 6.0, 2.8)


def draw_port_stiffness(key, part):
    return symmetric(key, 4 * P_SIZE, 6.0, 12.0, 4.0)


def touch_ends(values, own_key, low, top_value):
    longest = values.shape.index(max(values.shape))
    spots = []
    for shift in (0, 1):
        where = [jax.random.randint(jax.random.fold_in(own_key, axis), (), 0, length) for axis, length in enumerate(values.shape)]
        where[longest] = (where[longest] + shift) % values.shape[longest]
        spots.append(tuple(where))
    return values.at[spots[0]].set(low).at[spots[1]].set(top_value)


def level_of(stream_key, extent, cuts, least, high):
    def one(axis_at, shards_of):
        steps = jax.random.uniform(jax.random.fold_in(jax.random.fold_in(stream_key, 6), axis_at), (shards_of,), jnp.float32, least / len(cuts), high / len(cuts))
        return jnp.repeat(jnp.exp(steps), extent[axis_at] // shards_of).reshape((-1,) + (1,) * (len(extent) - axis_at - 1))

    loudness = one(*cuts[0])
    for cut in cuts[1:]:
        loudness = loudness * one(*cut)
    return loudness


def scatter_about(own_key, dims, deviation, limit, cuts=(), kind=jnp.bfloat16):
    entries = jax.random.normal(own_key, dims, jnp.float32) * deviation
    if len(cuts) > 0:
        entries = level_of(own_key, dims, cuts, -0.22, 0.18) * entries
    return jnp.clip(entries, min=-limit, max=limit).astype(kind)


def setup_inputs(seed: int = 0) -> dict:
    streams_of = jax.random.split(jax.random.key(seed), 10)
    instance_arch = touch_ends(jax.random.randint(streams_of[0], (NINST,), 0, NARCH), jax.random.fold_in(streams_of[0], 1), 0, NARCH - 1).astype(jnp.int32)
    instance_param = touch_ends(jax.random.randint(streams_of[1], (NINST,), 0, NPARAM), jax.random.fold_in(streams_of[1], 1), 0, NPARAM - 1).astype(jnp.int32)
    instance_ports = draw_instance_ports(jax.random.fold_in(streams_of[9], 71), 0)
    port_row = draw_port_row(jax.random.fold_in(streams_of[9], 71), 0)
    param_table = jnp.clip(jnp.exp(jax.random.uniform(streams_of[4], (NPARAM, M), jnp.float32, math.log(0.5), math.log(2.0))), 0.5, 2.0)
    bubble_inverse = draw_bubble_inverse(jax.random.fold_in(streams_of[9], 71), 0)
    coupling = scatter_about(streams_of[6], (NARCH, M, 4 * P_SIZE), M ** -0.5, 0.75, ((0, 4),), jnp.float32)
    port_stiffness = draw_port_stiffness(jax.random.fold_in(streams_of[9], 71), 0)
    coupling_offset = scatter_about(streams_of[8], (NINST, M, 4 * P_SIZE), (0.5 / M ** 0.5), 0.375, ((0, 128),), jnp.float32)
    return dict(instance_arch=instance_arch, instance_param=instance_param, instance_ports=instance_ports, port_row=port_row, param_table=param_table, bubble_inverse=bubble_inverse, coupling=coupling, port_stiffness=port_stiffness, coupling_offset=coupling_offset)


def orders(width):
    result = []
    for which in range(4):
        parts = [np.arange(which * width, (which + 1) * width)]
        for other in range(4):
            if other != which:
                parts.append(np.arange(other * width, (other + 1) * width))
        result.append(np.concatenate(parts))
    return result


def condense(inverses, couplings, stiffness, table, arch_ids, param_ids, offsets):
    scales = jnp.take(table, param_ids, axis=0)
    weighted = scales[:, :, None] * (jnp.take(couplings, arch_ids, axis=0) + offsets)
    applied = jnp.einsum("bmn,bnq->bmq", jnp.take(inverses, arch_ids, axis=0), weighted, precision=lax.Precision.HIGHEST)
    return jnp.take(stiffness, arch_ids, axis=0) - jnp.einsum("bmp,bmq->bpq", weighted, applied, precision=lax.Precision.HIGHEST)


def reference(instance_arch, instance_param, instance_ports, port_row, param_table, bubble_inverse, coupling, port_stiffness, coupling_offset):
    block_size = 256
    columns = orders(P_SIZE)
    diagonal = jnp.zeros((NPORTS, P_SIZE, P_SIZE), jnp.float32)
    even_part = jnp.zeros((NPORTS, P_SIZE, 3 * P_SIZE), jnp.float32)
    odd_part = jnp.zeros((NPORTS, P_SIZE, 3 * P_SIZE), jnp.float32)

    def advance(carry, number):
        diag_sum, even_rows, odd_rows = carry
        start = number * block_size
        arch_ids = lax.dynamic_slice_in_dim(instance_arch, start, block_size, 0)
        param_ids = lax.dynamic_slice_in_dim(instance_param, start, block_size, 0)
        port_ids = lax.dynamic_slice_in_dim(instance_ports, start, block_size, 0)
        offsets = lax.dynamic_slice_in_dim(coupling_offset, start, block_size, 0)
        schur = condense(bubble_inverse, coupling, port_stiffness, param_table, arch_ids, param_ids, offsets)
        row_ids = jnp.take(port_row, port_ids, axis=0)
        for which in range(4):
            strip = schur[:, which * P_SIZE:(which + 1) * P_SIZE, :][:, :, columns[which]]
            diag_sum = diag_sum.at[row_ids[:, which]].add(strip[:, :, :P_SIZE])
            if which % 2 == 0:
                even_rows = even_rows.at[row_ids[:, which]].set(strip[:, :, P_SIZE:])
            else:
                odd_rows = odd_rows.at[row_ids[:, which]].set(strip[:, :, P_SIZE:])
        return (diag_sum, even_rows, odd_rows), None

    numbers = jnp.arange(NINST // block_size, dtype=jnp.int32)
    (diagonal, even_part, odd_part), _ = lax.scan(advance, (diagonal, even_part, odd_part), numbers)
    return jnp.concatenate([diagonal, even_part, odd_part], axis=2).reshape(NPORTS, 7 * P_SIZE * P_SIZE)
```

```python
import functools

import jax
import jax.numpy as jnp
from jax import lax
from jax.experimental import pallas as pl
from jax.experimental.pallas import tpu as pltpu
from jax.sharding import PartitionSpec as P

MESH = pl.DeviceIdType.MESH
SIDE = 4
OFFSETS = (1, 3, 2)
LANES = 128
VMEM_LIMIT = 56 << 20


def position():
    inst, z = lax.axis_index("inst"), lax.axis_index("arch")
    return inst // (2 * SIDE), inst // 2 % SIDE, inst % 2, z


def device(x, y, core, z):
    return ((x * SIDE + y) * 2 + core, z)


def moved(here, axis, offset):
    there = list(here)
    there[axis] = (there[axis] + offset) % SIDE
    return tuple(there)


def greet(partners):
    barrier = pltpu.get_barrier_semaphore()
    for partner in partners:
        pl.semaphore_signal(barrier, inc=1, device_id=device(*partner), device_id_type=MESH)
    pl.semaphore_wait(barrier, len(partners))


def send(src, dst, send_sem, recv_sem, there):
    copy = pltpu.make_async_remote_copy(
        src, dst, send_sem, recv_sem, device_id=device(*there), device_id_type=MESH
    )
    copy.start()
    return copy


def take(ref, sem):
    pltpu.make_async_copy(ref, ref, sem).wait()


def gather_kernel(inverse, coupling, stiffness, basis, stiff, local, s1, r1, s2, r2, s3, r3):
    here = position()
    x, y, core, z = here
    other = (x, y, 1 - core, z)
    lines = [[moved(here, axis, o) for o in OFFSETS] for axis in (0, 1, 3)]
    greet([*lines[0], *lines[1], *lines[2], other])
    inverse_rows, basis_rows, stiff_rows = inverse.shape[0], basis.shape[1], stiff.shape[1]
    own = [
        pltpu.make_async_copy(inverse, basis.at[z, pl.ds(0, inverse_rows)], local.at[0]),
        pltpu.make_async_copy(
            coupling, basis.at[z, pl.ds(inverse_rows, basis_rows - inverse_rows)], local.at[1]
        ),
        pltpu.make_async_copy(stiffness, stiff.at[z], local.at[2]),
    ]
    for copy in own:
        copy.start()
    arrays = ((basis, (64, 56)), (stiff, (80, 80)))
    assert basis_rows == 8 * 120 and stiff_rows == 8 * 160

    def piece(ref, sizes, half, plane):
        size, base = sizes[half], half * 8 * sizes[0]
        return ref.at[plane, pl.ds(base + (core * SIDE + here[half]) * size, size)]

    def core_half(ref, sizes, half, plane, which):
        size, base = sizes[half], half * 8 * sizes[0]
        return ref.at[plane, pl.ds(base + which * SIDE * size, SIDE * size)]

    sent = []
    for a, (ref, sizes) in enumerate(arrays):
        for copy in own[:2] if a == 0 else own[2:]:
            copy.wait()
        for o, there in enumerate(lines[2]):
            for half in (0, 1):
                mine = piece(ref, sizes, half, z)
                sent.append(send(mine, mine, s1.at[a, o, half], r1.at[a, o, half], there))
    for a, (ref, sizes) in enumerate(arrays):
        for o, offset in enumerate(OFFSETS):
            plane = (z + SIDE - offset) % SIDE
            for half in (0, 1):
                got = piece(ref, sizes, half, plane)
                take(got, r1.at[a, o, half])
                for i, there in enumerate(lines[half]):
                    sent.append(send(got, got, s2.at[a, o, half, i], r2.at[a, o, half, i], there))
    for a, (ref, sizes) in enumerate(arrays):
        for o, offset in enumerate(OFFSETS):
            plane = (z + SIDE - offset) % SIDE
            for half in (0, 1):
                for i in range(3):
                    take(piece(ref, sizes, half, plane), r2.at[a, o, half, i])
                got = core_half(ref, sizes, half, plane, core)
                sent.append(send(got, got, s3.at[a, o, half], r3.at[a, o, half], other))
    for a, (ref, sizes) in enumerate(arrays):
        for o, offset in enumerate(OFFSETS):
            plane = (z + SIDE - offset) % SIDE
            for half in (0, 1):
                take(core_half(ref, sizes, half, plane, 1 - core), r3.at[a, o, half])
    for copy in sent:
        copy.wait_send()


def gather_bases(inverse, coupling, stiffness):
    dma = pltpu.SemaphoreType.DMA
    rows = inverse.shape[0] + coupling.shape[0]
    return pl.pallas_call(
        gather_kernel,
        out_shape=(
            jax.ShapeDtypeStruct((SIDE, rows, LANES), jnp.float32),
            jax.ShapeDtypeStruct((SIDE, stiffness.shape[0], LANES), jnp.float32),
        ),
        in_specs=[pl.BlockSpec(memory_space=pl.ANY)] * 3,
        out_specs=[pl.BlockSpec(memory_space=pl.ANY)] * 2,
        scratch_shapes=[
            dma((3,)),
            dma((2, 3, 2)),
            dma((2, 3, 2)),
            dma((2, 3, 2, 3)),
            dma((2, 3, 2, 3)),
            dma((2, 3, 2)),
            dma((2, 3, 2)),
        ],
        compiler_params=pltpu.CompilerParams(
            collective_id=0, has_side_effects=True, vmem_limit_bytes=VMEM_LIMIT
        ),
        name="gather_bases",
    )(inverse, coupling, stiffness)


def halves(value):
    high = value.astype(jnp.bfloat16).astype(jnp.float32)
    return high, value - high


def condense_kernel(arch, basis, stiff, scales, offset, strips, table):
    step = pl.program_id(0)
    block, modes = offset.shape[0], offset.shape[1]
    archs = stiff.shape[1] // LANES
    half = modes // 2
    lane = lax.broadcasted_iota(jnp.int32, (LANES, LANES), 1)
    left = lane < modes

    @pl.when(step == 0)
    def _():
        def one(a, carry):
            plane, at = a // archs, a % archs
            packed = basis[plane, pl.ds(pl.multiple_of(at * half, half), half), :]
            turned = pltpu.roll(packed, modes, 1)
            left_half = left[:half]
            both = jnp.concatenate(
                [jnp.where(left_half, packed, turned), jnp.where(left_half, turned, packed)], axis=0
            )
            high, low = halves(both)
            table[a] = jnp.concatenate([high, high, low, low], axis=0).astype(jnp.bfloat16)
            return carry

        lax.fori_loop(0, SIDE * archs, one, 0)

    lane8 = lane[: LANES // 4]
    for u in range(block):
        a = arch[step * block + u]
        plane, at = a // archs, a % archs
        start = pl.multiple_of(archs * half + at * modes, half)
        body = basis[plane, pl.ds(start, modes), :] + offset[u]
        weighted = jnp.concatenate([body, body], axis=0).T * scales[u : u + 1, :]
        high, low = halves(weighted)
        mixed = jnp.where(left, weighted, low).astype(jnp.bfloat16)
        applied = jnp.dot(
            jnp.concatenate([mixed, mixed], axis=1), table[a], preferred_element_type=jnp.float32
        )
        rest = halves(applied)[1]
        mixed = jnp.where(left, applied, rest).astype(jnp.bfloat16)
        product = lax.dot_general(
            jnp.concatenate([mixed, mixed], axis=1),
            jnp.concatenate([high.astype(jnp.bfloat16), low.astype(jnp.bfloat16)], axis=1),
            (((1,), (1,)), ((), ())),
            preferred_element_type=jnp.float32,
        )
        schur = stiff[plane, pl.ds(pl.multiple_of(at * LANES, LANES), LANES), :] - product
        for k in range(4):
            v = schur[k * 32 : (k + 1) * 32]
            if k > 0:
                first = pltpu.roll(v, LANES - 32 * k, 1)
                after = pltpu.roll(v, 32, 1)
                v = jnp.where(lane8 < 32, first, jnp.where(lane8 < 32 * (k + 1), after, v))
            strips[u, k] = v


def condense(arch, basis, stiff, scales, offset):
    block = 8
    instances, modes = offset.shape[0], offset.shape[1]
    count = SIDE * stiff.shape[1] // LANES
    return pl.pallas_call(
        condense_kernel,
        out_shape=jax.ShapeDtypeStruct((instances, 4, 32, LANES), jnp.float32),
        grid_spec=pltpu.PrefetchScalarGridSpec(
            num_scalar_prefetch=1,
            grid=(instances // block,),
            in_specs=[
                pl.BlockSpec(basis.shape, lambda i, a: (0, 0, 0), pipeline_mode=pl.Buffered(1)),
                pl.BlockSpec(stiff.shape, lambda i, a: (0, 0, 0), pipeline_mode=pl.Buffered(1)),
                pl.BlockSpec((block, LANES), lambda i, a: (i, 0)),
                pl.BlockSpec((block, modes, LANES), lambda i, a: (i, 0, 0)),
            ],
            out_specs=pl.BlockSpec((block, 4, 32, LANES), lambda i, a: (i, 0, 0, 0)),
            scratch_shapes=[pltpu.VMEM((count, 4 * modes, LANES), jnp.bfloat16)],
        ),
        compiler_params=pltpu.CompilerParams(vmem_limit_bytes=VMEM_LIMIT),
        name="condense",
    )(arch, basis, stiff, scales, offset)


ORDERS = ((0, 1, 3), (1, 3, 0), (3, 0, 1))


def exchange_kernel(slot_strip, slot_code, strips, arrived, first, second, third, local, ss, rs):
    here = position()
    core = here[2]
    other = (here[0], here[1], 1 - core, here[3])
    partners = [other]
    for axis in (0, 1, 3):
        for o in OFFSETS:
            there = moved(here, axis, o)
            partners += [there, (there[0], there[1], 1 - core, there[3])]
    greet(partners)
    row = lax.broadcasted_iota(jnp.int32, (8, LANES), 0)
    lane = lax.broadcasted_iota(jnp.int32, (8, LANES), 1)
    spot = (row == 1) & (lane == 0)

    def pack(part, line, into):
        def one(i, carry):
            at = part * 128 + line * 32 + i
            which = slot_strip[at]
            into[i // 8, i % 8, 8:] = strips[which, 8:]
            into[i // 8, i % 8, :8] = jnp.where(spot, slot_code[at], strips[which, :8])
            return carry

        lax.fori_loop(0, 32, one, 0, unroll=4)

    sent, copies = [], []
    for i, o in enumerate(OFFSETS):
        for part, (a1, a2, a3) in enumerate(ORDERS):
            line = (here[a1] + o) % SIDE
            pack(part, line, first.at[part, line])
            sent.append(
                send(
                    first.at[part, line],
                    second.at[part, here[a1]],
                    ss.at[part, 0, i],
                    rs.at[part, 0, i],
                    moved(here, a1, o),
                )
            )
    for part, (a1, a2, a3) in enumerate(ORDERS):
        pack(part, here[a1], second.at[part, here[a1]])
    for part, (a1, a2, a3) in enumerate(ORDERS):
        for i, o in enumerate(OFFSETS):
            take(second.at[part, 0], rs.at[part, 0, i])
        for i, o in enumerate(OFFSETS):
            line = (here[a2] + o) % SIDE
            sent.append(
                send(
                    second.at[part, :, line],
                    third.at[part, here[a2]],
                    ss.at[part, 1, i],
                    rs.at[part, 1, i],
                    moved(here, a2, o),
                )
            )
        copy = pltpu.make_async_copy(
            second.at[part, :, here[a2]], third.at[part, here[a2]], local.at[part, 0]
        )
        copy.start()
        copies.append(copy)
    for part, (a1, a2, a3) in enumerate(ORDERS):
        copies[part].wait()
        for i, o in enumerate(OFFSETS):
            take(third.at[part, 0], rs.at[part, 1, i])
        mine = here[a3] * 2 + core
        n = 2
        for o in (*OFFSETS, 0):
            for flip in (0, 1):
                there = moved(here, a3, o)
                to = (core + flip) % 2
                there = (there[0], there[1], to, there[3])
                src = third.at[part, :, :, there[a3] * 2 + to]
                dst = arrived.at[part, mine]
                if o == 0 and flip == 0:
                    copy = pltpu.make_async_copy(src, dst, local.at[part, 1])
                    copy.start()
                    copies.append(copy)
                else:
                    sent.append(send(src, dst, ss.at[part, 2, n - 2], rs.at[part, 2, n - 2], there))
                    n += 1
    for part in range(3):
        copies[3 + part].wait()
        for i in range(7):
            take(arrived.at[part, 0], rs.at[part, 2, i])
    for copy in sent:
        copy.wait_send()


def exchange(slot_strip, slot_code, strips):
    dma = pltpu.SemaphoreType.DMA
    return pl.pallas_call(
        exchange_kernel,
        out_shape=jax.ShapeDtypeStruct((3, 2 * SIDE, SIDE, SIDE, 32, LANES), jnp.float32),
        in_specs=[
            pl.BlockSpec(memory_space=pltpu.SMEM),
            pl.BlockSpec(memory_space=pltpu.SMEM),
            pl.BlockSpec(memory_space=pltpu.VMEM),
        ],
        out_specs=pl.BlockSpec(memory_space=pl.ANY),
        scratch_shapes=[
            pltpu.VMEM((3, SIDE, SIDE, 8, 32, LANES), jnp.float32),
            pltpu.VMEM((3, SIDE, SIDE, 8, 32, LANES), jnp.float32),
            pltpu.VMEM((3, SIDE, SIDE, 8, 32, LANES), jnp.float32),
            dma((3, 2)),
            dma((3, 3, 7)),
            dma((3, 3, 7)),
        ],
        compiler_params=pltpu.CompilerParams(
            collective_id=1, has_side_effects=True, vmem_limit_bytes=VMEM_LIMIT
        ),
        name="exchange",
    )(slot_strip, slot_code, strips)


def assemble_kernel(where, arrived, out, even, odd, sems):
    step, steps = pl.program_id(0), pl.num_programs(0)

    def copies(at, slot):
        for r in range(8):
            for parity, buffer in enumerate((even, odd)):
                yield pltpu.make_async_copy(
                    arrived.at[where[(at * 8 + r) * 2 + parity]],
                    buffer.at[slot, pl.ds(r * 32, 32)],
                    sems.at[slot, parity, r],
                )

    @pl.when(step == 0)
    def _():
        for copy in copies(0, 0):
            copy.start()

    @pl.when(step + 1 < steps)
    def _():
        for copy in copies(step + 1, (step + 1) % 2):
            copy.start()

    slot = step % 2
    for copy in copies(step, slot):
        copy.wait()
    lane = lax.broadcasted_iota(jnp.int32, (8, LANES), 1)

    def row(i):
        e = even[slot, pl.ds(i, 8, stride=32), :]
        o = odd[slot, pl.ds(i, 8, stride=32), :]
        return jnp.where(lane < 32, e + o, e), o

    for g in range(8):
        (s0, o0), (s1, o1), (s2, o2), (s3, o3) = (row(4 * g + i) for i in range(4))
        if g == 0:
            s1 = jnp.where(lane == 0, pltpu.roll(s0, LANES - 1, 1), s1)
        tiles = (
            s0,
            pltpu.roll(jnp.where(lane < 32, s1, o0), 96, 1),
            jnp.where(lane < 96, pltpu.roll(s1, 96, 1), pltpu.roll(o1, 64, 1)),
            pltpu.roll(jnp.where(lane < 64, s2, o1), 64, 1),
            jnp.where(lane < 64, pltpu.roll(s2, 64, 1), pltpu.roll(o2, 32, 1)),
            pltpu.roll(jnp.where(lane < 96, s3, o2), 32, 1),
            jnp.where(lane < 32, pltpu.roll(s3, 32, 1), o3),
        )
        for t, tile in enumerate(tiles):
            out[:, (7 * g + t) * LANES : (7 * g + t + 1) * LANES] = tile


def assemble(where, arrived, ports):
    return pl.pallas_call(
        assemble_kernel,
        out_shape=jax.ShapeDtypeStruct((ports, 56 * LANES), jnp.float32),
        grid_spec=pltpu.PrefetchScalarGridSpec(
            num_scalar_prefetch=1,
            grid=(ports // 8,),
            in_specs=[pl.BlockSpec(memory_space=pl.ANY)],
            out_specs=pl.BlockSpec((8, 56 * LANES), lambda i, w: (i, 0)),
            scratch_shapes=[
                pltpu.VMEM((2, 8 * 32, LANES), jnp.float32),
                pltpu.VMEM((2, 8 * 32, LANES), jnp.float32),
                pltpu.SemaphoreType.DMA((2, 2, 8)),
            ],
        ),
        compiler_params=pltpu.CompilerParams(vmem_limit_bytes=VMEM_LIMIT),
        name="assemble",
    )(where, arrived)


def body(
    instance_arch,
    instance_param,
    instance_ports,
    port_row,
    param_table,
    bubble_inverse,
    coupling,
    port_stiffness,
    coupling_offset,
):
    instances = instance_arch.shape[0]
    ports = 2 * instances
    archs, modes = bubble_inverse.shape[:2]
    packed = jnp.concatenate(
        [bubble_inverse[:, : modes // 2], bubble_inverse[:, modes // 2 :]], axis=2
    )
    basis, stiff = gather_bases(
        packed.reshape(archs * modes // 2, LANES),
        coupling.reshape(archs * modes, LANES),
        port_stiffness.reshape(archs * LANES, LANES),
    )
    scales = jnp.take(param_table, instance_param, axis=0)
    scales = jnp.concatenate([scales, scales], axis=1)

    count = 4 * instances
    strip = jnp.arange(count, dtype=jnp.int32)
    rows = jnp.take(port_row, instance_ports.reshape(count), axis=0)
    owner = rows // ports
    code = rows % ports * 2 + strip % 2
    earlier = (owner[:, None] == owner[None, :]) & (strip[None, :] < strip[:, None])
    ordinal = jnp.sum(earlier.astype(jnp.int32), axis=1)
    z, core, y, x = owner % 4, owner // 4 % 2, owner // 8 % 4, owner // 32
    place = jnp.where(
        ordinal == 0,
        (x * 4 + y) * 8 + z * 2 + core,
        jnp.where(ordinal == 1, 128 + (y * 4 + z) * 8 + x * 2 + core, 256 + (z * 4 + x) * 8 + y * 2 + core),
    )
    slots = jnp.arange(384, dtype=jnp.int32)
    chosen = place[None, :] == slots[:, None]
    slot_strip = jnp.sum(jnp.where(chosen, strip[None, :], 0), axis=1)
    slot_code = jnp.sum(jnp.where(chosen, code[None, :] + 1, 0), axis=1).astype(jnp.float32) - 1.0

    strips = condense(instance_arch, basis, stiff, scales, coupling_offset)
    arrived = exchange(slot_strip, slot_code, strips.reshape(count, 32, LANES))
    arrived = arrived.reshape(384, 32, LANES)
    codes = arrived[:, 1, 0]
    wanted = jnp.arange(2 * ports, dtype=jnp.int32).astype(jnp.float32)
    where = jnp.sum(jnp.where(codes[None, :] == wanted[:, None], slots[None, :], 0), axis=1)
    return assemble(where, arrived, ports)


def solution(mesh):
    return jax.shard_map(
        body,
        mesh=mesh,
        in_specs=(
            P(("inst", "arch")),
            P(("inst", "arch")),
            P(("inst", "arch"), None),
            P(),
            P(),
            P("arch", None, None),
            P("arch", None, None),
            P("arch", None, None),
            P(("inst", "arch"), None, None),
        ),
        out_specs=P(("inst", "arch"), None),
        check_vma=False,
    )
```

```python
import functools

import jax
import jax.numpy as jnp
from jax import lax
from jax.experimental import pallas as pl
from jax.experimental.pallas import tpu as pltpu
from jax.sharding import PartitionSpec as P

MESH = pl.DeviceIdType.MESH
SIDE = 4
OFFSETS = (1, 3, 2)
LANES = 128
VMEM_LIMIT = 56 << 20


def position():
    inst, z = lax.axis_index("inst"), lax.axis_index("arch")
    return inst // (2 * SIDE), inst // 2 % SIDE, inst % 2, z


def device(x, y, core, z):
    return ((x * SIDE + y) * 2 + core, z)


def moved(here, axis, offset):
    there = list(here)
    there[axis] = (there[axis] + offset) % SIDE
    return tuple(there)


def greet(partners):
    barrier = pltpu.get_barrier_semaphore()
    for partner in partners:
        pl.semaphore_signal(barrier, inc=1, device_id=device(*partner), device_id_type=MESH)
    pl.semaphore_wait(barrier, len(partners))


def send(src, dst, send_sem, recv_sem, there):
    copy = pltpu.make_async_remote_copy(
        src, dst, send_sem, recv_sem, device_id=device(*there), device_id_type=MESH
    )
    copy.start()
    return copy


def take(ref, sem):
    pltpu.make_async_copy(ref, ref, sem).wait()


PIECES = ((64, 56), (80, 80))
ORDERS = ((0, 1, 3), (1, 3, 0), (3, 0, 1))


def halves(value):
    high = value.astype(jnp.bfloat16).astype(jnp.float32)
    return high, value - high


def reorder(v, k):
    if k == 0:
        return v
    lane = lax.broadcasted_iota(jnp.int32, v.shape, 1)
    first = pltpu.roll(v, LANES - 32 * k, 1)
    after = pltpu.roll(v, 32, 1)
    return jnp.where(lane < 32, first, jnp.where(lane < 32 * (k + 1), after, v))


def strips_kernel(
    arch,
    param,
    ports,
    row_in,
    params_in,
    inverse_in,
    coupling_in,
    stiffness_in,
    offset_in,
    arrived_out,
    where,
    arrived,
    inverse,
    basis,
    stiff,
    offset,
    turned,
    inverse_table,
    natural,
    coupling_table,
    stiff_table,
    strips,
    scales,
    params,
    rows,
    slots_vector,
    slots,
    first,
    second,
    third,
    local,
    s1,
    r1,
    s2,
    r2,
    s3,
    r3,
    here_sems,
    out_sems,
    ss,
    rs,
):
    here = position()
    x, y, core, z = here
    other = (x, y, 1 - core, z)
    lines = {axis: [moved(here, axis, o) for o in OFFSETS] for axis in (0, 1, 3)}
    archs, modes = inverse.shape[0], inverse.shape[1]
    instances = offset.shape[0]
    half_modes = modes // 2
    inverse_rows, coupling_rows = archs * half_modes, archs * modes
    own = [
        pltpu.make_async_copy(inverse_in, inverse, local.at[0]),
        pltpu.make_async_copy(coupling_in, basis.at[z, pl.ds(inverse_rows, coupling_rows)], local.at[1]),
        pltpu.make_async_copy(stiffness_in, stiff.at[z], local.at[2]),
        pltpu.make_async_copy(offset_in, offset, local.at[3]),
        pltpu.make_async_copy(row_in, rows, local.at[4]),
        pltpu.make_async_copy(params_in, params, local.at[5]),
    ]
    for copy in own:
        copy.start()
    partners = [other]
    for axis in (0, 1, 3):
        for there in lines[axis]:
            partners += [there, (there[0], there[1], 1 - core, there[3])]
    greet(partners)

    lane = lax.broadcasted_iota(jnp.int32, (LANES, LANES), 1)
    left = lane < modes
    left_half = left[:half_modes]
    row8 = lax.broadcasted_iota(jnp.int32, (8, LANES), 0)
    lane8 = lane[:8]

    own[0].wait()
    for a in range(archs):
        top = jnp.concatenate([inverse[a, :half_modes], inverse[a, half_modes:]], axis=1)
        basis[z, a * half_modes : (a + 1) * half_modes] = top
    own[1].wait()
    arrays = ((basis, PIECES[0]), (stiff, PIECES[1]))

    def piece(a, half, plane):
        ref, sizes = arrays[a]
        size, base = sizes[half], half * 8 * sizes[0]
        return ref.at[plane, pl.ds(base + (core * SIDE + here[half]) * size, size)]

    def core_half(a, half, plane, which):
        ref, sizes = arrays[a]
        size, base = sizes[half], half * 8 * sizes[0]
        return ref.at[plane, pl.ds(base + which * SIDE * size, SIDE * size)]

    sent = []
    planes = [(z + SIDE - o) % SIDE for o in OFFSETS]

    def along_z(a):
        for o, there in enumerate(lines[3]):
            for half in (0, 1):
                mine = piece(a, half, z)
                sent.append(send(mine, mine, s1.at[a, o, half], r1.at[a, o, half], there))

    def along_lines(a):
        for o, plane in enumerate(planes):
            for half in (0, 1):
                got = piece(a, half, plane)
                take(got, r1.at[a, o, half])
                for i, there in enumerate(lines[half]):
                    sent.append(send(got, got, s2.at[a, o, half, i], r2.at[a, o, half, i], there))

    def to_other_core(a):
        for o, plane in enumerate(planes):
            for half in (0, 1):
                for i in range(3):
                    take(piece(a, half, plane), r2.at[a, o, half, i])
                got = core_half(a, half, plane, core)
                sent.append(send(got, got, s3.at[a, o, half], r3.at[a, o, half], other))

    def wait_plane(a, o):
        for half in (0, 1):
            take(core_half(a, half, planes[o], 1 - core), r3.at[a, o, half])

    def basis_tables(plane):
        def one(at, carry):
            packed = basis[plane, pl.ds(pl.multiple_of(at * half_modes, half_modes), half_modes), :]
            flipped = pltpu.roll(packed, modes, 1)
            both = jnp.concatenate(
                [jnp.where(left_half, packed, flipped), jnp.where(left_half, flipped, packed)], axis=0
            )
            high, low = halves(both)
            inverse_table[plane * archs + at] = jnp.concatenate([high, high, low, low], axis=0).astype(
                jnp.bfloat16
            )
            begin = pl.multiple_of(inverse_rows + at * modes, half_modes)
            c = basis[plane, pl.ds(begin, modes), :]
            natural[plane * archs + at] = c
            coupling_table[plane * archs + at] = jnp.concatenate([c, c], axis=0).T
            return carry

        lax.fori_loop(0, archs, one, 0, unroll=2)

    def stiff_tables(plane):
        def one(at, carry):
            for k in range(4):
                begin = pl.multiple_of(at * LANES + k * 32, 32)
                stiff_table[(plane * archs + at) * 4 + k] = reorder(stiff[plane, pl.ds(begin, 32), :], k)
            return carry

        lax.fori_loop(0, archs, one, 0)

    def turn(begin, end):
        def one(i, carry):
            v = offset[i]
            turned[i] = jnp.concatenate([v, v], axis=0).T
            return carry

        lax.fori_loop(begin, end, one, 0, unroll=2)

    def look_up_scales():
        wanted = jnp.zeros((8, LANES), jnp.int32)
        for i in range(instances):
            wanted = jnp.where(lane8 == i, param[i], wanted)
        samples = params.shape[1]
        sample = lax.broadcasted_iota(jnp.int32, (samples, LANES), 0)
        chosen = jnp.where(sample == wanted[:1], 1.0, 0.0).astype(jnp.bfloat16)
        high, rest = halves(params[...])
        middle, low = halves(rest)
        found = jnp.zeros((modes, LANES), jnp.float32)
        for part in (high, middle, low):
            found = found + jnp.dot(part.astype(jnp.bfloat16), chosen, preferred_element_type=jnp.float32)
        scales[...] = jnp.concatenate([found, found], axis=0).T[:instances]

    def place_strips():
        def one(i, carry):
            low, high = carry
            low = jnp.where(lane8 == i, rows[ports[0, i]], low)
            low = jnp.where(lane8 == i + instances, rows[ports[1, i]], low)
            high = jnp.where(lane8 == i, rows[ports[2, i]], high)
            high = jnp.where(lane8 == i + instances, rows[ports[3, i]], high)
            return low, high

        zero = jnp.zeros((8, LANES), jnp.int32)
        row = lax.fori_loop(0, instances, one, (zero, zero), unroll=8)

        def down(v):
            return jnp.broadcast_to(v[:1], (LANES, LANES)).T

        wanted = jnp.zeros((8, LANES), jnp.int32)
        for i in range(instances):
            wanted = jnp.where((lane8 == i) | (lane8 == i + instances), arch[i] * 4, wanted)
        sub = lax.broadcasted_iota(jnp.int32, (LANES, LANES), 0)
        owner = [v >> 7 for v in row]
        owner_down = [down(v) for v in owner]
        places, values = [], []
        for h in (0, 1):
            across = owner[h][:1]
            same = jnp.where((owner_down[h] == across) & (sub < lane), 1, 0)
            if h == 1:
                same = same + jnp.where(owner_down[0] == across, 1, 0)
            ordinal = jnp.sum(same, axis=0, keepdims=True)
            oz, oc, oy, ox = across & 3, (across >> 2) & 1, (across >> 3) & 3, across >> 5
            place = jnp.where(
                ordinal == 0,
                (ox * 4 + oy) * 8 + oz * 2 + oc,
                jnp.where(
                    ordinal == 1,
                    128 + (oy * 4 + oz) * 8 + ox * 2 + oc,
                    256 + (oz * 4 + ox) * 8 + oy * 2 + oc,
                ),
            )
            odd = jnp.where(lane8[:1] < instances, 0, 1)
            code = (row[h][:1] & 127) * 2 + odd
            stiff_at = wanted[:1] + odd + 2 * h
            places.append(down(place))
            values.append(down((stiff_at << 17) + ((code + 1) << 8) + lane8[:1] + h * LANES))
        for j in range(3):
            target = lane8[:1] + j * LANES
            total = jnp.zeros((LANES, LANES), jnp.int32)
            for h in (0, 1):
                total = jnp.maximum(total, jnp.where(places[h] == target, values[h], 0))
            value = jnp.max(total, axis=0, keepdims=True)
            slots_vector[j : j + 1] = value & 255
            slots_vector[j + 3 : j + 4] = ((value >> 8) & 511) - 1
            slots_vector[j + 6 : j + 7] = value >> 17

    along_z(0)
    own[2].wait()
    own[4].wait()
    place_strips()
    to_scalars = pltpu.make_async_copy(slots_vector, slots, local.at[6])
    to_scalars.start()
    along_lines(0)
    along_z(1)
    own[3].wait()
    own[5].wait()
    look_up_scales()
    basis_tables(z)
    to_other_core(0)
    turn(0, instances // 2)
    along_lines(1)
    turn(instances // 2, instances)
    stiff_tables(z)
    for o in range(3):
        wait_plane(0, o)
        basis_tables(planes[o])
    to_other_core(1)

    def condense(step, carry):
        for u in range(4):
            i = step * 4 + u
            a = arch[i]
            scale = scales[pl.ds(i, 1), :]
            weighted = (coupling_table[a] + turned[i]) * scale
            mixed = jnp.where(left, weighted, halves(weighted)[1]).astype(jnp.bfloat16)
            applied = scale * jnp.dot(
                jnp.concatenate([mixed, mixed], axis=1),
                inverse_table[a],
                preferred_element_type=jnp.float32,
            )
            mixed = jnp.where(left, applied, halves(applied)[1]).astype(jnp.bfloat16)
            high, low = halves(natural[a] + offset[i])
            product = jnp.dot(
                jnp.concatenate([mixed, mixed], axis=1),
                jnp.concatenate([high, high, low, low], axis=0).astype(jnp.bfloat16),
                preferred_element_type=jnp.float32,
            )
            for k in range(4):
                strips[k * instances + i] = reorder(product[k * 32 : (k + 1) * 32], k)
        return carry

    lax.fori_loop(0, instances // 4, condense, 0)
    for o in range(3):
        wait_plane(1, o)
        stiff_tables(planes[o])

    to_scalars.wait()
    spot = (row8 == 1) & (lane8 == 0)

    def pack(part, line, into):
        def one(i, carry):
            at = line * 32 + i
            strip = slots[part, at]
            stiff_at = slots[part + 6, at]
            into[i // 8, i % 8, 8:] = stiff_table[stiff_at, 8:] - strips[strip, 8:]
            top = stiff_table[stiff_at, :8] - strips[strip, :8]
            into[i // 8, i % 8, :8] = jnp.where(spot, slots[part + 3, at].astype(jnp.float32), top)
            return carry

        lax.fori_loop(0, 32, one, 0, unroll=4)

    copies = []
    for i, o in enumerate(OFFSETS):
        for part, (a1, a2, a3) in enumerate(ORDERS):
            line = (here[a1] + o) % SIDE
            pack(part, line, first.at[part, line])
            sent.append(
                send(
                    first.at[part, line],
                    second.at[part, here[a1]],
                    ss.at[part, 0, i],
                    rs.at[part, 0, i],
                    moved(here, a1, o),
                )
            )
    for part, (a1, a2, a3) in enumerate(ORDERS):
        pack(part, here[a1], second.at[part, here[a1]])
    for part, (a1, a2, a3) in enumerate(ORDERS):
        for i, o in enumerate(OFFSETS):
            take(second.at[part, 0], rs.at[part, 0, i])
        for i, o in enumerate(OFFSETS):
            line = (here[a2] + o) % SIDE
            sent.append(
                send(
                    second.at[part, :, line],
                    third.at[part, here[a2]],
                    ss.at[part, 1, i],
                    rs.at[part, 1, i],
                    moved(here, a2, o),
                )
            )
        copy = pltpu.make_async_copy(
            second.at[part, :, here[a2]], third.at[part, here[a2]], here_sems.at[part, 0]
        )
        copy.start()
        copies.append(copy)
    for part, (a1, a2, a3) in enumerate(ORDERS):
        copies[part].wait()
        for i, o in enumerate(OFFSETS):
            take(third.at[part, 0], rs.at[part, 1, i])
        mine = here[a3] * 2 + core
        n = 0
        for o in (*OFFSETS, 0):
            for flip in (0, 1):
                there = moved(here, a3, o)
                to = (core + flip) % 2
                there = (there[0], there[1], to, there[3])
                src = third.at[part, :, :, there[a3] * 2 + to]
                dst = arrived.at[part, mine]
                if o == 0 and flip == 0:
                    copy = pltpu.make_async_copy(src, dst, here_sems.at[part, 1])
                    copy.start()
                    copies.append(copy)
                else:
                    sent.append(send(src, dst, ss.at[part, 2, n], rs.at[part, 2, n], there))
                    n += 1
    out = []
    for part, (a1, a2, a3) in enumerate(ORDERS):
        mine = here[a3] * 2 + core
        n = 0
        for o in (0, *OFFSETS):
            for flip in (0, 1):
                origin = (here[a3] + SIDE - o) % SIDE * 2 + (core + flip) % 2
                if o == 0 and flip == 0:
                    copies[3 + part].wait()
                else:
                    take(arrived.at[part, origin], rs.at[part, 2, (n + 6) % 7])
                    n += 1
                copy = pltpu.make_async_copy(
                    arrived.at[part, origin], arrived_out.at[part, origin], out_sems.at[part, n]
                )
                copy.start()
                out.append(copy)
    landed = arrived.reshape(384 * 32, LANES)
    found = [jnp.zeros((8, LANES), jnp.int32)] * 2
    for g in range(48):
        codes = landed[pl.ds(g * 256 + 1, 8, stride=32), :][:, :1]
        for t in (0, 1):
            hit = codes == (lane8 + t * LANES).astype(jnp.float32)
            found[t] = found[t] + jnp.where(hit, row8 + g * 8, 0)
    for t in (0, 1):
        where[t : t + 1, :] = jnp.sum(found[t], axis=0, keepdims=True)
    for copy in sent:
        copy.wait_send()
    for copy in out:
        copy.wait()


def strips_of(arch, param, ports, rows, params, inverse, coupling, stiffness, offset):
    dma = pltpu.SemaphoreType.DMA
    archs, modes = inverse.shape[:2]
    instances, count = offset.shape[0], SIDE * archs
    f32 = jnp.float32
    assert archs * modes * 3 // 2 == 8 * sum(PIECES[0]) and archs * LANES == 8 * sum(PIECES[1])
    smem, vmem, anywhere = (
        pl.BlockSpec(memory_space=m) for m in (pltpu.SMEM, pltpu.VMEM, pl.ANY)
    )
    return pl.pallas_call(
        strips_kernel,
        out_shape=(
            jax.ShapeDtypeStruct((3, 2 * SIDE, SIDE, SIDE, 32, LANES), f32),
            jax.ShapeDtypeStruct((2, LANES), jnp.int32),
        ),
        in_specs=[smem] * 3 + [anywhere] * 6,
        out_specs=[anywhere, vmem],
        scratch_shapes=[
            pltpu.VMEM((3, 2 * SIDE, SIDE, SIDE, 32, LANES), f32),
            pltpu.VMEM(inverse.shape, f32),
            pltpu.VMEM((SIDE, archs * modes * 3 // 2, LANES), f32),
            pltpu.VMEM((SIDE, archs * LANES, LANES), f32),
            pltpu.VMEM(offset.shape, f32),
            pltpu.VMEM((instances, LANES, LANES), f32),
            pltpu.VMEM((count, 4 * modes, LANES), jnp.bfloat16),
            pltpu.VMEM((count, modes, LANES), f32),
            pltpu.VMEM((count, LANES, LANES), f32),
            pltpu.VMEM((count * 4, 32, LANES), f32),
            pltpu.VMEM((instances * 4, 32, LANES), f32),
            pltpu.VMEM((instances, LANES), f32),
            pltpu.VMEM(params.shape, f32),
            pltpu.SMEM(rows.shape, jnp.int32),
            pltpu.VMEM((16, LANES), jnp.int32),
            pltpu.SMEM((16, LANES), jnp.int32),
            pltpu.VMEM((3, SIDE, SIDE, 8, 32, LANES), f32),
            pltpu.VMEM((3, SIDE, SIDE, 8, 32, LANES), f32),
            pltpu.VMEM((3, SIDE, SIDE, 8, 32, LANES), f32),
            dma((7,)),
            dma((2, 3, 2)),
            dma((2, 3, 2)),
            dma((2, 3, 2, 3)),
            dma((2, 3, 2, 3)),
            dma((2, 3, 2)),
            dma((2, 3, 2)),
            dma((3, 2)),
            dma((3, 8)),
            dma((3, 3, 7)),
            dma((3, 3, 7)),
        ],
        compiler_params=pltpu.CompilerParams(
            collective_id=0, has_side_effects=True, vmem_limit_bytes=VMEM_LIMIT
        ),
        name="strips",
    )(arch, param, ports, rows, params, inverse, coupling, stiffness, offset)


AHEAD = 5


def assemble_kernel(where, arrived, out, even, odd, sems):
    step, steps = pl.program_id(0), pl.num_programs(0)

    def copies(at, slot):
        for r in range(8):
            for parity, buffer in enumerate((even, odd)):
                yield pltpu.make_async_copy(
                    arrived.at[where[(at * 8 + r) * 2 + parity]],
                    buffer.at[slot, pl.ds(r * 32, 32)],
                    sems.at[slot, parity, r],
                )

    @pl.when(step == 0)
    def _():
        for ahead in range(AHEAD):
            for copy in copies(ahead, ahead):
                copy.start()

    @pl.when(step + AHEAD < steps)
    def _():
        for copy in copies(step + AHEAD, (step + AHEAD) % (AHEAD + 1)):
            copy.start()

    slot = step % (AHEAD + 1)
    for copy in copies(step, slot):
        copy.wait()
    lane = lax.broadcasted_iota(jnp.int32, (8, LANES), 1)

    def row(i):
        e = even[slot, pl.ds(i, 8, stride=32), :]
        o = odd[slot, pl.ds(i, 8, stride=32), :]
        return jnp.where(lane < 32, e + o, e), o

    for g in range(8):
        (s0, o0), (s1, o1), (s2, o2), (s3, o3) = (row(4 * g + i) for i in range(4))
        if g == 0:
            s1 = jnp.where(lane == 0, pltpu.roll(s0, LANES - 1, 1), s1)
        tiles = (
            s0,
            pltpu.roll(jnp.where(lane < 32, s1, o0), 96, 1),
            jnp.where(lane < 96, pltpu.roll(s1, 96, 1), pltpu.roll(o1, 64, 1)),
            pltpu.roll(jnp.where(lane < 64, s2, o1), 64, 1),
            jnp.where(lane < 64, pltpu.roll(s2, 64, 1), pltpu.roll(o2, 32, 1)),
            pltpu.roll(jnp.where(lane < 96, s3, o2), 32, 1),
            jnp.where(lane < 32, pltpu.roll(s3, 32, 1), o3),
        )
        for t, tile in enumerate(tiles):
            out[:, (7 * g + t) * LANES : (7 * g + t + 1) * LANES] = tile


def assemble(where, arrived, ports):
    return pl.pallas_call(
        assemble_kernel,
        out_shape=jax.ShapeDtypeStruct((ports, 56 * LANES), jnp.float32),
        grid_spec=pltpu.PrefetchScalarGridSpec(
            num_scalar_prefetch=1,
            grid=(ports // 8,),
            in_specs=[pl.BlockSpec(memory_space=pl.ANY)],
            out_specs=pl.BlockSpec((8, 56 * LANES), lambda i, w: (i, 0)),
            scratch_shapes=[
                pltpu.VMEM((AHEAD + 1, 8 * 32, LANES), jnp.float32),
                pltpu.VMEM((AHEAD + 1, 8 * 32, LANES), jnp.float32),
                pltpu.SemaphoreType.DMA((AHEAD + 1, 2, 8)),
            ],
        ),
        compiler_params=pltpu.CompilerParams(vmem_limit_bytes=VMEM_LIMIT),
        name="assemble",
    )(where, arrived)


def body(
    instance_arch,
    instance_param,
    instance_ports,
    port_row,
    param_table,
    bubble_inverse,
    coupling,
    port_stiffness,
    coupling_offset,
):
    instances = instance_arch.shape[0]
    ports = 2 * instances
    archs, modes = coupling.shape[:2]
    arrived, where = strips_of(
        instance_arch,
        instance_param,
        instance_ports.T,
        port_row,
        param_table.T,
        bubble_inverse,
        coupling.reshape(archs * modes, LANES),
        port_stiffness.reshape(archs * LANES, LANES),
        coupling_offset,
    )
    return assemble(where.reshape(2 * ports), arrived.reshape(384, 32, LANES), ports)


def solution(mesh):
    return jax.shard_map(
        body,
        mesh=mesh,
        in_specs=(
            P(("inst", "arch")),
            P(("inst", "arch")),
            P(("inst", "arch"), None),
            P(),
            P(),
            P("arch", None, None),
            P("arch", None, None),
            P("arch", None, None),
            P(("inst", "arch"), None, None),
        ),
        out_specs=P(("inst", "arch"), None),
        check_vma=False,
    )
```

```python
import functools

import jax
import jax.numpy as jnp
from jax import lax
from jax.experimental import pallas as pl
from jax.experimental.pallas import tpu as pltpu
from jax.sharding import PartitionSpec as P

MESH = pl.DeviceIdType.MESH
SIDE = 4
OFFSETS = (1, 3, 2)
LANES = 128
VMEM_LIMIT = 56 << 20
UNROLL = 16


def position():
    inst, z = lax.axis_index("inst"), lax.axis_index("arch")
    return inst // (2 * SIDE), inst // 2 % SIDE, inst % 2, z


def device(x, y, core, z):
    return ((x * SIDE + y) * 2 + core, z)


def moved(here, axis, offset):
    there = list(here)
    there[axis] = (there[axis] + offset) % SIDE
    return tuple(there)


def greet(partners):
    barrier = pltpu.get_barrier_semaphore()
    for partner in partners:
        pl.semaphore_signal(barrier, inc=1, device_id=device(*partner), device_id_type=MESH)
    pl.semaphore_wait(barrier, len(partners))


def send(src, dst, send_sem, recv_sem, there):
    copy = pltpu.make_async_remote_copy(
        src, dst, send_sem, recv_sem, device_id=device(*there), device_id_type=MESH
    )
    copy.start()
    return copy


def take(ref, sem):
    pltpu.make_async_copy(ref, ref, sem).wait()


PIECES = ((64, 56), (80, 80))
ORDERS = ((0, 1, 3), (1, 3, 0), (3, 0, 1))


def halves(value):
    high = value.astype(jnp.bfloat16).astype(jnp.float32)
    return high, value - high


def reorder(v, k):
    if k == 0:
        return v
    lane = lax.broadcasted_iota(jnp.int32, v.shape, 1)
    first = pltpu.roll(v, LANES - 32 * k, 1)
    after = pltpu.roll(v, 32, 1)
    return jnp.where(lane < 32, first, jnp.where(lane < 32 * (k + 1), after, v))


def strips_kernel(
    arch,
    param,
    ports,
    row_in,
    params_in,
    inverse_in,
    coupling_in,
    stiffness_in,
    offset_in,
    arrived_out,
    where,
    arrived,
    inverse,
    basis,
    stiff,
    offset,
    turned,
    inverse_table,
    natural,
    coupling_table,
    stiff_table,
    strips,
    scales,
    params,
    rows,
    slots_vector,
    slots,
    first,
    second,
    third,
    local,
    s1,
    r1,
    s2,
    r2,
    s3,
    r3,
    here_sems,
    out_sems,
    ss,
    rs,
):
    here = position()
    x, y, core, z = here
    other = (x, y, 1 - core, z)
    lines = {axis: [moved(here, axis, o) for o in OFFSETS] for axis in (0, 1, 3)}
    archs, modes = inverse.shape[0], inverse.shape[1]
    instances = offset.shape[0]
    half_modes = modes // 2
    inverse_rows, coupling_rows = archs * half_modes, archs * modes
    own = [
        pltpu.make_async_copy(inverse_in, inverse, local.at[0]),
        pltpu.make_async_copy(coupling_in, basis.at[z, pl.ds(inverse_rows, coupling_rows)], local.at[1]),
        pltpu.make_async_copy(stiffness_in, stiff.at[z], local.at[2]),
        pltpu.make_async_copy(offset_in, offset, local.at[3]),
        pltpu.make_async_copy(row_in, rows, local.at[4]),
        pltpu.make_async_copy(params_in, params, local.at[5]),
    ]
    for copy in own:
        copy.start()
    partners = [other]
    for axis in (0, 1, 3):
        for there in lines[axis]:
            partners += [there, (there[0], there[1], 1 - core, there[3])]
    greet(partners)

    lane = lax.broadcasted_iota(jnp.int32, (LANES, LANES), 1)
    left = lane < modes
    left_half = left[:half_modes]
    row8 = lax.broadcasted_iota(jnp.int32, (8, LANES), 0)
    lane8 = lane[:8]

    own[0].wait()
    for a in range(archs):
        top = jnp.concatenate([inverse[a, :half_modes], inverse[a, half_modes:]], axis=1)
        basis[z, a * half_modes : (a + 1) * half_modes] = top
    own[1].wait()
    arrays = ((basis, PIECES[0]), (stiff, PIECES[1]))

    def piece(a, half, plane):
        ref, sizes = arrays[a]
        size, base = sizes[half], half * 8 * sizes[0]
        return ref.at[plane, pl.ds(base + (core * SIDE + here[half]) * size, size)]

    def core_half(a, half, plane, which):
        ref, sizes = arrays[a]
        size, base = sizes[half], half * 8 * sizes[0]
        return ref.at[plane, pl.ds(base + which * SIDE * size, SIDE * size)]

    sent = []
    planes = [(z + SIDE - o) % SIDE for o in OFFSETS]

    def along_z(a):
        for o, there in enumerate(lines[3]):
            for half in (0, 1):
                mine = piece(a, half, z)
                sent.append(send(mine, mine, s1.at[a, o, half], r1.at[a, o, half], there))

    def along_lines(a):
        for o, plane in enumerate(planes):
            for half in (0, 1):
                got = piece(a, half, plane)
                take(got, r1.at[a, o, half])
                for i, there in enumerate(lines[half]):
                    sent.append(send(got, got, s2.at[a, o, half, i], r2.at[a, o, half, i], there))

    def to_other_core(a):
        for o, plane in enumerate(planes):
            for half in (0, 1):
                for i in range(3):
                    take(piece(a, half, plane), r2.at[a, o, half, i])
                got = core_half(a, half, plane, core)
                sent.append(send(got, got, s3.at[a, o, half], r3.at[a, o, half], other))

    def wait_plane(a, o):
        for half in (0, 1):
            take(core_half(a, half, planes[o], 1 - core), r3.at[a, o, half])

    def basis_tables(plane):
        def one(at, carry):
            packed = basis[plane, pl.ds(pl.multiple_of(at * half_modes, half_modes), half_modes), :]
            flipped = pltpu.roll(packed, modes, 1)
            both = jnp.concatenate(
                [jnp.where(left_half, packed, flipped), jnp.where(left_half, flipped, packed)], axis=0
            )
            inverse_table[plane * archs + at] = both
            begin = pl.multiple_of(inverse_rows + at * modes, half_modes)
            c = basis[plane, pl.ds(begin, modes), :]
            natural[plane * archs + at] = c
            coupling_table[plane * archs + at] = jnp.concatenate([c, c], axis=0).T
            return carry

        lax.fori_loop(0, archs, one, 0, unroll=2)

    def stiff_tables(plane):
        def one(at, carry):
            for k in range(4):
                begin = pl.multiple_of(at * LANES + k * 32, 32)
                stiff_table[(plane * archs + at) * 4 + k] = reorder(stiff[plane, pl.ds(begin, 32), :], k)
            return carry

        lax.fori_loop(0, archs, one, 0, unroll=5)

    def turn(begin, end):
        def one(i, carry):
            v = offset[i]
            turned[i] = jnp.concatenate([v, v], axis=0).T
            return carry

        lax.fori_loop(begin, end, one, 0, unroll=2)

    def look_up_scales():
        wanted = jnp.zeros((8, LANES), jnp.int32)
        for i in range(instances):
            wanted = jnp.where(lane8 == i, param[i], wanted)
        samples = params.shape[1]
        sample = lax.broadcasted_iota(jnp.int32, (samples, LANES), 0)
        chosen = jnp.where(sample == wanted[:1], 1.0, 0.0).astype(jnp.bfloat16)
        high, rest = halves(params[...])
        middle, low = halves(rest)
        found = jnp.zeros((modes, LANES), jnp.float32)
        for part in (high, middle, low):
            found = found + jnp.dot(part.astype(jnp.bfloat16), chosen, preferred_element_type=jnp.float32)
        scales[...] = jnp.concatenate([found, found], axis=0).T[:instances]

    def place_strips():
        def one(i, carry):
            low, high = carry
            low = jnp.where(lane8 == i, rows[ports[0, i]], low)
            low = jnp.where(lane8 == i + instances, rows[ports[1, i]], low)
            high = jnp.where(lane8 == i, rows[ports[2, i]], high)
            high = jnp.where(lane8 == i + instances, rows[ports[3, i]], high)
            return low, high

        zero = jnp.zeros((8, LANES), jnp.int32)
        row = lax.fori_loop(0, instances, one, (zero, zero), unroll=8)

        def down(v):
            return jnp.broadcast_to(v[:1], (LANES, LANES)).T

        wanted = jnp.zeros((8, LANES), jnp.int32)
        for i in range(instances):
            wanted = jnp.where((lane8 == i) | (lane8 == i + instances), arch[i] * 4, wanted)
        sub = lax.broadcasted_iota(jnp.int32, (LANES, LANES), 0)
        owner = [v >> 7 for v in row]
        owner_down = [down(v) for v in owner]
        places, values = [], []
        for h in (0, 1):
            across = owner[h][:1]
            same = jnp.where((owner_down[h] == across) & (sub < lane), 1, 0)
            if h == 1:
                same = same + jnp.where(owner_down[0] == across, 1, 0)
            ordinal = jnp.sum(same, axis=0, keepdims=True)
            oz, oc, oy, ox = across & 3, (across >> 2) & 1, (across >> 3) & 3, across >> 5
            place = jnp.where(
                ordinal == 0,
                (ox * 4 + oy) * 8 + oz * 2 + oc,
                jnp.where(
                    ordinal == 1,
                    128 + (oy * 4 + oz) * 8 + ox * 2 + oc,
                    256 + (oz * 4 + ox) * 8 + oy * 2 + oc,
                ),
            )
            odd = jnp.where(lane8[:1] < instances, 0, 1)
            code = (row[h][:1] & 127) * 2 + odd
            stiff_at = wanted[:1] + odd + 2 * h
            places.append(down(place))
            values.append(down((stiff_at << 17) + ((code + 1) << 8) + lane8[:1] + h * LANES))
        for j in range(3):
            target = lane8[:1] + j * LANES
            total = jnp.zeros((LANES, LANES), jnp.int32)
            for h in (0, 1):
                total = jnp.maximum(total, jnp.where(places[h] == target, values[h], 0))
            value = jnp.max(total, axis=0, keepdims=True)
            slots_vector[j : j + 1] = value & 255
            slots_vector[j + 3 : j + 4] = ((value >> 8) & 511) - 1
            slots_vector[j + 6 : j + 7] = value >> 17

    along_z(0)
    own[2].wait()
    own[4].wait()
    place_strips()
    to_scalars = pltpu.make_async_copy(slots_vector, slots, local.at[6])
    to_scalars.start()
    along_lines(0)
    along_z(1)
    own[3].wait()
    own[5].wait()
    turn(0, instances)
    basis_tables(z)
    look_up_scales()
    to_other_core(0)
    along_lines(1)
    for o in range(3):
        wait_plane(0, o)
        basis_tables(planes[o])
    to_other_core(1)

    left_modes = left[:modes]

    def condense(step, carry):
        applied = []
        for u in range(UNROLL):
            i = step * UNROLL + u
            a = arch[i]
            scaled = inverse_table[a] * scales[pl.ds(i, 1), :]
            mixed = jnp.where(left_modes, scaled, halves(scaled)[1]).astype(jnp.bfloat16)
            high, low = halves(natural[a] + offset[i])
            applied.append(
                jnp.dot(
                    jnp.concatenate([mixed, mixed], axis=1),
                    jnp.concatenate([high, high, low, low], axis=0).astype(jnp.bfloat16),
                    preferred_element_type=jnp.float32,
                )
            )
        for u in range(UNROLL):
            i = step * UNROLL + u
            high, low = halves(applied[u])
            weighted = (coupling_table[arch[i]] + turned[i]) * scales[pl.ds(i, 1), :]
            mixed = jnp.where(left, weighted, halves(weighted)[1]).astype(jnp.bfloat16)
            product = jnp.dot(
                jnp.concatenate([mixed, mixed], axis=1),
                jnp.concatenate([high, high, low, low], axis=0).astype(jnp.bfloat16),
                preferred_element_type=jnp.float32,
            )
            for k in range(4):
                strips[k * instances + i] = reorder(product[k * 32 : (k + 1) * 32], k)
        return carry

    lax.fori_loop(0, instances // UNROLL, condense, 0)
    stiff_tables(z)
    for o in range(3):
        wait_plane(1, o)
        stiff_tables(planes[o])

    to_scalars.wait()
    spot = (row8 == 1) & (lane8 == 0)

    def pack(part, line, into):
        def one(i, carry):
            at = line * 32 + i
            strip = slots[part, at]
            stiff_at = slots[part + 6, at]
            into[i // 8, i % 8, 8:] = stiff_table[stiff_at, 8:] - strips[strip, 8:]
            top = stiff_table[stiff_at, :8] - strips[strip, :8]
            into[i // 8, i % 8, :8] = jnp.where(spot, slots[part + 3, at].astype(jnp.float32), top)
            return carry

        lax.fori_loop(0, 32, one, 0, unroll=4)

    copies = []
    for i, o in enumerate(OFFSETS):
        for part, (a1, a2, a3) in enumerate(ORDERS):
            line = (here[a1] + o) % SIDE
            pack(part, line, first.at[part, line])
            sent.append(
                send(
                    first.at[part, line],
                    second.at[part, here[a1]],
                    ss.at[part, 0, i],
                    rs.at[part, 0, i],
                    moved(here, a1, o),
                )
            )
    for part, (a1, a2, a3) in enumerate(ORDERS):
        pack(part, here[a1], second.at[part, here[a1]])
    for part, (a1, a2, a3) in enumerate(ORDERS):
        for i, o in enumerate(OFFSETS):
            take(second.at[part, 0], rs.at[part, 0, i])
        for i, o in enumerate(OFFSETS):
            line = (here[a2] + o) % SIDE
            sent.append(
                send(
                    second.at[part, :, line],
                    third.at[part, here[a2]],
                    ss.at[part, 1, i],
                    rs.at[part, 1, i],
                    moved(here, a2, o),
                )
            )
        copy = pltpu.make_async_copy(
            second.at[part, :, here[a2]], third.at[part, here[a2]], here_sems.at[part, 0]
        )
        copy.start()
        copies.append(copy)
    for part, (a1, a2, a3) in enumerate(ORDERS):
        copies[part].wait()
        for i, o in enumerate(OFFSETS):
            take(third.at[part, 0], rs.at[part, 1, i])
        mine = here[a3] * 2 + core
        n = 0
        for o in (*OFFSETS, 0):
            for flip in (0, 1):
                there = moved(here, a3, o)
                to = (core + flip) % 2
                there = (there[0], there[1], to, there[3])
                src = third.at[part, :, :, there[a3] * 2 + to]
                dst = arrived.at[part, mine]
                if o == 0 and flip == 0:
                    copy = pltpu.make_async_copy(src, dst, here_sems.at[part, 1])
                    copy.start()
                    copies.append(copy)
                else:
                    sent.append(send(src, dst, ss.at[part, 2, n], rs.at[part, 2, n], there))
                    n += 1
    out = []
    for part, (a1, a2, a3) in enumerate(ORDERS):
        mine = here[a3] * 2 + core
        n = 0
        for o in (0, *OFFSETS):
            for flip in (0, 1):
                origin = (here[a3] + SIDE - o) % SIDE * 2 + (core + flip) % 2
                if o == 0 and flip == 0:
                    copies[3 + part].wait()
                else:
                    take(arrived.at[part, origin], rs.at[part, 2, (n + 6) % 7])
                    n += 1
                copy = pltpu.make_async_copy(
                    arrived.at[part, origin], arrived_out.at[part, origin], out_sems.at[part, n]
                )
                copy.start()
                out.append(copy)
    landed = arrived.reshape(384 * 32, LANES)
    found = [jnp.zeros((8, LANES), jnp.int32)] * 2
    for g in range(48):
        codes = landed[pl.ds(g * 256 + 1, 8, stride=32), :][:, :1]
        for t in (0, 1):
            hit = codes == (lane8 + t * LANES).astype(jnp.float32)
            found[t] = found[t] + jnp.where(hit, row8 + g * 8, 0)
    for t in (0, 1):
        where[t : t + 1, :] = jnp.sum(found[t], axis=0, keepdims=True)
    for copy in sent:
        copy.wait_send()
    for copy in out:
        copy.wait()


def strips_of(arch, param, ports, rows, params, inverse, coupling, stiffness, offset):
    dma = pltpu.SemaphoreType.DMA
    archs, modes = inverse.shape[:2]
    instances, count = offset.shape[0], SIDE * archs
    f32 = jnp.float32
    assert archs * modes * 3 // 2 == 8 * sum(PIECES[0]) and archs * LANES == 8 * sum(PIECES[1])
    smem, vmem, anywhere = (
        pl.BlockSpec(memory_space=m) for m in (pltpu.SMEM, pltpu.VMEM, pl.ANY)
    )
    return pl.pallas_call(
        strips_kernel,
        out_shape=(
            jax.ShapeDtypeStruct((3, 2 * SIDE, SIDE, SIDE, 32, LANES), f32),
            jax.ShapeDtypeStruct((2, LANES), jnp.int32),
        ),
        in_specs=[smem] * 3 + [anywhere] * 6,
        out_specs=[anywhere, vmem],
        scratch_shapes=[
            pltpu.VMEM((3, 2 * SIDE, SIDE, SIDE, 32, LANES), f32),
            pltpu.VMEM(inverse.shape, f32),
            pltpu.VMEM((SIDE, archs * modes * 3 // 2, LANES), f32),
            pltpu.VMEM((SIDE, archs * LANES, LANES), f32),
            pltpu.VMEM(offset.shape, f32),
            pltpu.VMEM((instances, LANES, LANES), f32),
            pltpu.VMEM((count, modes, LANES), f32),
            pltpu.VMEM((count, modes, LANES), f32),
            pltpu.VMEM((count, LANES, LANES), f32),
            pltpu.VMEM((count * 4, 32, LANES), f32),
            pltpu.VMEM((instances * 4, 32, LANES), f32),
            pltpu.VMEM((instances, LANES), f32),
            pltpu.VMEM(params.shape, f32),
            pltpu.SMEM(rows.shape, jnp.int32),
            pltpu.VMEM((16, LANES), jnp.int32),
            pltpu.SMEM((16, LANES), jnp.int32),
            pltpu.VMEM((3, SIDE, SIDE, 8, 32, LANES), f32),
            pltpu.VMEM((3, SIDE, SIDE, 8, 32, LANES), f32),
            pltpu.VMEM((3, SIDE, SIDE, 8, 32, LANES), f32),
            dma((7,)),
            dma((2, 3, 2)),
            dma((2, 3, 2)),
            dma((2, 3, 2, 3)),
            dma((2, 3, 2, 3)),
            dma((2, 3, 2)),
            dma((2, 3, 2)),
            dma((3, 2)),
            dma((3, 8)),
            dma((3, 3, 7)),
            dma((3, 3, 7)),
        ],
        compiler_params=pltpu.CompilerParams(
            collective_id=0, has_side_effects=True, vmem_limit_bytes=VMEM_LIMIT
        ),
        name="strips",
    )(arch, param, ports, rows, params, inverse, coupling, stiffness, offset)


AHEAD = 12


def assemble_kernel(where, arrived, out, even, odd, rows, in_sems, out_sems):
    groups = rows.shape[0]

    def fetch(group):
        for r in range(8):
            for parity, buffer in enumerate((even, odd)):
                pltpu.make_async_copy(
                    arrived.at[where[(group * 8 + r) * 2 + parity]],
                    buffer.at[group, :, r],
                    in_sems.at[group, parity],
                ).start()

    def written(group):
        begin = pl.multiple_of(group * 8, 8)
        return pltpu.make_async_copy(rows.at[group], out.at[pl.ds(begin, 8)], out_sems.at[group])

    lane = lax.broadcasted_iota(jnp.int32, (8, LANES), 1)
    for group in range(AHEAD):
        fetch(group)

    def lay_out(group, carry):
        @pl.when(group + AHEAD < groups)
        def _():
            fetch(group + AHEAD)

        take(even.at[group], in_sems.at[group, 0])
        take(odd.at[group], in_sems.at[group, 1])

        def row(i):
            e, o = even[group, i], odd[group, i]
            return jnp.where(lane < 32, e + o, e), o

        for g in range(8):
            (s0, o0), (s1, o1), (s2, o2), (s3, o3) = (row(4 * g + i) for i in range(4))
            if g == 0:
                s1 = jnp.where(lane == 0, pltpu.roll(s0, LANES - 1, 1), s1)
            tiles = (
                s0,
                pltpu.roll(jnp.where(lane < 32, s1, o0), 96, 1),
                jnp.where(lane < 96, pltpu.roll(s1, 96, 1), pltpu.roll(o1, 64, 1)),
                pltpu.roll(jnp.where(lane < 64, s2, o1), 64, 1),
                jnp.where(lane < 64, pltpu.roll(s2, 64, 1), pltpu.roll(o2, 32, 1)),
                pltpu.roll(jnp.where(lane < 96, s3, o2), 32, 1),
                jnp.where(lane < 32, pltpu.roll(s3, 32, 1), o3),
            )
            for t, tile in enumerate(tiles):
                rows[group, :, (7 * g + t) * LANES : (7 * g + t + 1) * LANES] = tile
        written(group).start()
        return carry

    lax.fori_loop(0, groups, lay_out, 0)

    def finish(group, carry):
        written(group).wait()
        return carry

    lax.fori_loop(0, groups, finish, 0)


def assemble(where, arrived, ports):
    groups = ports // 8
    return pl.pallas_call(
        assemble_kernel,
        out_shape=jax.ShapeDtypeStruct((ports, 56 * LANES), jnp.float32),
        in_specs=[pl.BlockSpec(memory_space=pltpu.SMEM), pl.BlockSpec(memory_space=pl.ANY)],
        out_specs=pl.BlockSpec(memory_space=pl.ANY),
        scratch_shapes=[
            pltpu.VMEM((groups, 32, 8, LANES), jnp.float32),
            pltpu.VMEM((groups, 32, 8, LANES), jnp.float32),
            pltpu.VMEM((groups, 8, 56 * LANES), jnp.float32),
            pltpu.SemaphoreType.DMA((groups, 2)),
            pltpu.SemaphoreType.DMA((groups,)),
        ],
        compiler_params=pltpu.CompilerParams(vmem_limit_bytes=VMEM_LIMIT),
        name="assemble",
    )(where, arrived)


def body(
    instance_arch,
    instance_param,
    instance_ports,
    port_row,
    param_table,
    bubble_inverse,
    coupling,
    port_stiffness,
    coupling_offset,
):
    instances = instance_arch.shape[0]
    ports = 2 * instances
    archs, modes = coupling.shape[:2]
    arrived, where = strips_of(
        instance_arch,
        instance_param,
        instance_ports.T,
        port_row,
        param_table.T,
        bubble_inverse,
        coupling.reshape(archs * modes, LANES),
        port_stiffness.reshape(archs * LANES, LANES),
        coupling_offset,
    )
    return assemble(where.reshape(2 * ports), arrived.reshape(384, 32, LANES), ports)


def solution(mesh):
    return jax.shard_map(
        body,
        mesh=mesh,
        in_specs=(
            P(("inst", "arch")),
            P(("inst", "arch")),
            P(("inst", "arch"), None),
            P(),
            P(),
            P("arch", None, None),
            P("arch", None, None),
            P("arch", None, None),
            P(("inst", "arch"), None, None),
        ),
        out_specs=P(("inst", "arch"), None),
        check_vma=False,
    )
```

```python
import functools

import jax
import jax.numpy as jnp
from jax import lax
from jax.experimental import pallas as pl
from jax.experimental.pallas import tpu as pltpu
from jax.sharding import PartitionSpec as P

MESH = pl.DeviceIdType.MESH
SIDE = 4
OFFSETS = (1, 3, 2)
LANES = 128
VMEM_LIMIT = 56 << 20
UNROLL = 16


def position():
    inst, z = lax.axis_index("inst"), lax.axis_index("arch")
    return inst // (2 * SIDE), inst // 2 % SIDE, inst % 2, z


def device(x, y, core, z):
    return ((x * SIDE + y) * 2 + core, z)


def moved(here, axis, offset):
    there = list(here)
    there[axis] = (there[axis] + offset) % SIDE
    return tuple(there)


def greet(partners):
    barrier = pltpu.get_barrier_semaphore()
    for partner in partners:
        pl.semaphore_signal(barrier, inc=1, device_id=device(*partner), device_id_type=MESH)
    pl.semaphore_wait(barrier, len(partners))


def send(src, dst, send_sem, recv_sem, there):
    copy = pltpu.make_async_remote_copy(
        src, dst, send_sem, recv_sem, device_id=device(*there), device_id_type=MESH
    )
    copy.start()
    return copy


def take(ref, sem):
    pltpu.make_async_copy(ref, ref, sem).wait()


PIECES = ((64, 56), (80, 80))
ORDERS = ((0, 1, 3), (1, 3, 0), (3, 0, 1))


def halves(value):
    high = value.astype(jnp.bfloat16).astype(jnp.float32)
    return high, value - high


def reorder(v, k):
    if k == 0:
        return v
    lane = lax.broadcasted_iota(jnp.int32, v.shape, 1)
    first = pltpu.roll(v, LANES - 32 * k, 1)
    after = pltpu.roll(v, 32, 1)
    return jnp.where(lane < 32, first, jnp.where(lane < 32 * (k + 1), after, v))


def strips_kernel(
    arch,
    param,
    ports,
    row_in,
    params_in,
    inverse_in,
    coupling_in,
    stiffness_in,
    offset_in,
    arrived_out,
    where,
    arrived,
    inverse,
    basis,
    stiff,
    offset,
    turned,
    inverse_table,
    natural,
    coupling_table,
    stiff_table,
    strips,
    scales,
    params,
    rows,
    slots_vector,
    slots,
    first,
    second,
    third,
    local,
    s1,
    r1,
    s2,
    r2,
    s3,
    r3,
    here_sems,
    out_sems,
    ss1,
    ss2,
    ss3,
    rs,
):
    here = position()
    x, y, core, z = here
    other = (x, y, 1 - core, z)
    lines = {axis: [moved(here, axis, o) for o in OFFSETS] for axis in (0, 1, 3)}
    archs, modes = inverse.shape[0], inverse.shape[1]
    instances = offset.shape[0]
    half_modes = modes // 2
    inverse_rows, coupling_rows = archs * half_modes, archs * modes
    own = [
        pltpu.make_async_copy(inverse_in, inverse, local.at[0]),
        pltpu.make_async_copy(coupling_in, basis.at[z, pl.ds(inverse_rows, coupling_rows)], local.at[1]),
        pltpu.make_async_copy(stiffness_in, stiff.at[z], local.at[2]),
        pltpu.make_async_copy(offset_in, offset, local.at[3]),
        pltpu.make_async_copy(row_in, rows, local.at[4]),
        pltpu.make_async_copy(params_in, params, local.at[5]),
    ]
    for copy in own:
        copy.start()
    partners = [other]
    for axis in (0, 1, 3):
        for there in lines[axis]:
            partners += [there, (there[0], there[1], 1 - core, there[3])]
    greet(partners)

    lane = lax.broadcasted_iota(jnp.int32, (LANES, LANES), 1)
    left = lane < modes
    left_half = left[:half_modes]
    row8 = lax.broadcasted_iota(jnp.int32, (8, LANES), 0)
    lane8 = lane[:8]

    own[0].wait()
    for a in range(archs):
        top = jnp.concatenate([inverse[a, :half_modes], inverse[a, half_modes:]], axis=1)
        basis[z, a * half_modes : (a + 1) * half_modes] = top
    own[1].wait()
    arrays = ((basis, PIECES[0]), (stiff, PIECES[1]))

    def piece(a, half, plane):
        ref, sizes = arrays[a]
        size, base = sizes[half], half * 8 * sizes[0]
        return ref.at[plane, pl.ds(base + (core * SIDE + here[half]) * size, size)]

    def core_half(a, half, plane, which):
        ref, sizes = arrays[a]
        size, base = sizes[half], half * 8 * sizes[0]
        return ref.at[plane, pl.ds(base + which * SIDE * size, SIDE * size)]

    sent = []
    planes = [(z + SIDE - o) % SIDE for o in OFFSETS]

    def along_z(a):
        for o, there in enumerate(lines[3]):
            for half in (0, 1):
                mine = piece(a, half, z)
                sent.append(send(mine, mine, s1.at[a, o, half], r1.at[a, o, half], there))

    def along_lines(a):
        for o, plane in enumerate(planes):
            for half in (0, 1):
                got = piece(a, half, plane)
                take(got, r1.at[a, o, half])
                for i, there in enumerate(lines[half]):
                    sent.append(send(got, got, s2.at[a, o, half, i], r2.at[a, o, half, i], there))

    def to_other_core(a):
        for o, plane in enumerate(planes):
            for half in (0, 1):
                for i in range(3):
                    take(piece(a, half, plane), r2.at[a, o, half, i])
                got = core_half(a, half, plane, core)
                sent.append(send(got, got, s3.at[a, o, half], r3.at[a, o, half], other))

    def wait_plane(a, o):
        for half in (0, 1):
            take(core_half(a, half, planes[o], 1 - core), r3.at[a, o, half])

    def basis_tables(plane):
        def one(at, carry):
            packed = basis[plane, pl.ds(pl.multiple_of(at * half_modes, half_modes), half_modes), :]
            flipped = pltpu.roll(packed, modes, 1)
            both = jnp.concatenate(
                [jnp.where(left_half, packed, flipped), jnp.where(left_half, flipped, packed)], axis=0
            )
            inverse_table[plane * archs + at] = both
            begin = pl.multiple_of(inverse_rows + at * modes, half_modes)
            c = basis[plane, pl.ds(begin, modes), :]
            natural[plane * archs + at] = c
            coupling_table[plane * archs + at] = jnp.concatenate([c, c], axis=0).T
            return carry

        lax.fori_loop(0, archs, one, 0, unroll=5)

    def stiff_tables(plane):
        def one(at, carry):
            for k in range(4):
                begin = pl.multiple_of(at * LANES + k * 32, 32)
                stiff_table[(plane * archs + at) * 4 + k] = reorder(stiff[plane, pl.ds(begin, 32), :], k)
            return carry

        lax.fori_loop(0, archs, one, 0, unroll=5)

    def turn(begin, end):
        def one(i, carry):
            v = offset[i]
            turned[i] = jnp.concatenate([v, v], axis=0).T
            return carry

        lax.fori_loop(begin, end, one, 0, unroll=8)

    def look_up_scales():
        wanted = jnp.zeros((8, LANES), jnp.int32)
        for i in range(instances):
            wanted = jnp.where(lane8 == i, param[i], wanted)
        samples = params.shape[1]
        sample = lax.broadcasted_iota(jnp.int32, (samples, LANES), 0)
        chosen = jnp.where(sample == wanted[:1], 1.0, 0.0).astype(jnp.bfloat16)
        high, rest = halves(params[...])
        middle, low = halves(rest)
        found = jnp.zeros((modes, LANES), jnp.float32)
        for part in (high, middle, low):
            found = found + jnp.dot(part.astype(jnp.bfloat16), chosen, preferred_element_type=jnp.float32)
        scales[...] = jnp.concatenate([found, found], axis=0).T[:instances]

    def place_strips():
        def one(i, carry):
            low, high = carry
            low = jnp.where(lane8 == i, rows[ports[0, i]], low)
            low = jnp.where(lane8 == i + instances, rows[ports[1, i]], low)
            high = jnp.where(lane8 == i, rows[ports[2, i]], high)
            high = jnp.where(lane8 == i + instances, rows[ports[3, i]], high)
            return low, high

        zero = jnp.zeros((8, LANES), jnp.int32)
        row = lax.fori_loop(0, instances, one, (zero, zero), unroll=8)

        def down(v):
            return jnp.broadcast_to(v[:1], (LANES, LANES)).T

        wanted = jnp.zeros((8, LANES), jnp.int32)
        for i in range(instances):
            wanted = jnp.where((lane8 == i) | (lane8 == i + instances), arch[i] * 4, wanted)
        sub = lax.broadcasted_iota(jnp.int32, (LANES, LANES), 0)
        owner = [v >> 7 for v in row]
        owner_down = [down(v) for v in owner]
        places, values = [], []
        for h in (0, 1):
            across = owner[h][:1]
            same = jnp.where((owner_down[h] == across) & (sub < lane), 1, 0)
            if h == 1:
                same = same + jnp.where(owner_down[0] == across, 1, 0)
            ordinal = jnp.sum(same, axis=0, keepdims=True)
            oz, oc, oy, ox = across & 3, (across >> 2) & 1, (across >> 3) & 3, across >> 5
            place = jnp.where(
                ordinal == 0,
                (ox * 4 + oy) * 8 + oz * 2 + oc,
                jnp.where(
                    ordinal == 1,
                    128 + (oy * 4 + oz) * 8 + ox * 2 + oc,
                    256 + (oz * 4 + ox) * 8 + oy * 2 + oc,
                ),
            )
            odd = jnp.where(lane8[:1] < instances, 0, 1)
            code = (row[h][:1] & 127) * 2 + odd
            stiff_at = wanted[:1] + odd + 2 * h
            places.append(down(place))
            values.append(down((stiff_at << 17) + ((code + 1) << 8) + lane8[:1] + h * LANES))
        for j in range(3):
            target = lane8[:1] + j * LANES
            total = jnp.zeros((LANES, LANES), jnp.int32)
            for h in (0, 1):
                total = jnp.maximum(total, jnp.where(places[h] == target, values[h], 0))
            value = jnp.max(total, axis=0, keepdims=True)
            slots_vector[j : j + 1] = value & 255
            slots_vector[j + 3 : j + 4] = ((value >> 8) & 511) - 1
            slots_vector[j + 6 : j + 7] = value >> 17

    along_z(0)
    own[2].wait()
    own[4].wait()
    place_strips()
    to_scalars = pltpu.make_async_copy(slots_vector, slots, local.at[6])
    to_scalars.start()
    along_lines(0)
    along_z(1)
    own[3].wait()
    own[5].wait()
    turn(0, instances)
    basis_tables(z)
    look_up_scales()
    to_other_core(0)
    along_lines(1)
    for o in range(3):
        wait_plane(0, o)
        basis_tables(planes[o])
    to_other_core(1)

    left_modes = left[:modes]

    def condense(step, carry):
        applied = []
        for u in range(UNROLL):
            i = step * UNROLL + u
            a = arch[i]
            scaled = inverse_table[a] * scales[pl.ds(i, 1), :]
            mixed = jnp.where(left_modes, scaled, halves(scaled)[1]).astype(jnp.bfloat16)
            high, low = halves(natural[a] + offset[i])
            applied.append(
                jnp.dot(
                    jnp.concatenate([mixed, mixed], axis=1),
                    jnp.concatenate([high, high, low, low], axis=0).astype(jnp.bfloat16),
                    preferred_element_type=jnp.float32,
                )
            )
        for u in range(UNROLL):
            i = step * UNROLL + u
            high, low = halves(applied[u])
            weighted = (coupling_table[arch[i]] + turned[i]) * scales[pl.ds(i, 1), :]
            mixed = jnp.where(left, weighted, halves(weighted)[1]).astype(jnp.bfloat16)
            product = jnp.dot(
                jnp.concatenate([mixed, mixed], axis=1),
                jnp.concatenate([high, high, low, low], axis=0).astype(jnp.bfloat16),
                preferred_element_type=jnp.float32,
            )
            for k in range(4):
                strips[k * instances + i] = reorder(product[k * 32 : (k + 1) * 32], k)
        return carry

    lax.fori_loop(0, instances // UNROLL, condense, 0)
    stiff_tables(z)
    for o in range(3):
        wait_plane(1, o)
        stiff_tables(planes[o])

    to_scalars.wait()
    spot = (row8 == 1) & (lane8 == 0)

    def pack(part, line, into):
        def one(i, carry):
            at = line * 32 + i
            strip = slots[part, at]
            stiff_at = slots[part + 6, at]
            into[i // 8, i % 8, 8:] = stiff_table[stiff_at, 8:] - strips[strip, 8:]
            top = stiff_table[stiff_at, :8] - strips[strip, :8]
            into[i // 8, i % 8, :8] = jnp.where(spot, slots[part + 3, at].astype(jnp.float32), top)
            return carry

        lax.fori_loop(0, 32, one, 0, unroll=8)

    for i, o in enumerate(OFFSETS):
        for part, (a1, a2, a3) in enumerate(ORDERS):
            line = (here[a1] + o) % SIDE
            pack(part, line, first.at[part, line])
            there = moved(here, a1, o)
            sent.append(
                send(
                    first.at[part, line],
                    second.at[part, here[a1]],
                    ss1.at[part, i],
                    rs.at[part, 0, i],
                    there,
                )
            )
    for part, (a1, a2, a3) in enumerate(ORDERS):
        pack(part, here[a1], second.at[part, here[a1]])
    kept = [[], [], []]
    for n, o in enumerate((0, *OFFSETS)):
        for part, (a1, a2, a3) in enumerate(ORDERS):
            source = (here[a1] + SIDE - o) % SIDE
            if o:
                take(second.at[part, source], rs.at[part, 0, n - 1])
            dst = third.at[part, here[a2], source]
            for i, p in enumerate(OFFSETS):
                there = moved(here, a2, p)
                src = second.at[part, source, there[a2]]
                sent.append(send(src, dst, ss2.at[part, i, n], rs.at[part, 1, i], there))
            copy = pltpu.make_async_copy(
                second.at[part, source, here[a2]], dst, here_sems.at[part, 0, n]
            )
            copy.start()
            kept[part].append(copy)
    own_strips = [[], [], []]
    for n, o in enumerate((0, *OFFSETS)):
        for part, (a1, a2, a3) in enumerate(ORDERS):
            source = (here[a2] + SIDE - o) % SIDE
            if o:
                take(third.at[part, source], rs.at[part, 1, n - 1])
            else:
                for copy in kept[part]:
                    copy.wait()
            dst = arrived.at[part, here[a3] * 2 + core, source]
            i = 0
            for p in (*OFFSETS, 0):
                for flip in (0, 1):
                    there = moved(here, a3, p)
                    to = (core + flip) % 2
                    there = (there[0], there[1], to, there[3])
                    src = third.at[part, source, :, there[a3] * 2 + to]
                    if p == 0 and flip == 0:
                        copy = pltpu.make_async_copy(src, dst, here_sems.at[part, 1, n])
                        copy.start()
                        own_strips[part].append(copy)
                    else:
                        sent.append(send(src, dst, ss3.at[part, i, n], rs.at[part, 2, i], there))
                        i += 1
    out = []
    for n, (o, flip) in enumerate([(o, flip) for o in (0, *OFFSETS) for flip in (0, 1)]):
        for part, (a1, a2, a3) in enumerate(ORDERS):
            origin = (here[a3] + SIDE - o) % SIDE * 2 + (core + flip) % 2
            if n == 0:
                for copy in own_strips[part]:
                    copy.wait()
            else:
                take(arrived.at[part, origin], rs.at[part, 2, (n + 5) % 7])
            copy = pltpu.make_async_copy(
                arrived.at[part, origin], arrived_out.at[part, origin], out_sems.at[part, n]
            )
            copy.start()
            out.append(copy)
    landed = arrived.reshape(384 * 32, LANES)
    found = [jnp.zeros((8, LANES), jnp.int32)] * 2
    for g in range(48):
        codes = landed[pl.ds(g * 256 + 1, 8, stride=32), :][:, :1]
        for t in (0, 1):
            hit = codes == (lane8 + t * LANES).astype(jnp.float32)
            found[t] = found[t] + jnp.where(hit, row8 + g * 8, 0)
    for t in (0, 1):
        where[t : t + 1, :] = jnp.sum(found[t], axis=0, keepdims=True)
    for copy in sent:
        copy.wait_send()
    for copy in out:
        copy.wait()


def strips_of(arch, param, ports, rows, params, inverse, coupling, stiffness, offset):
    dma = pltpu.SemaphoreType.DMA
    archs, modes = inverse.shape[:2]
    instances, count = offset.shape[0], SIDE * archs
    f32 = jnp.float32
    assert archs * modes * 3 // 2 == 8 * sum(PIECES[0]) and archs * LANES == 8 * sum(PIECES[1])
    smem, vmem, anywhere = (
        pl.BlockSpec(memory_space=m) for m in (pltpu.SMEM, pltpu.VMEM, pl.ANY)
    )
    return pl.pallas_call(
        strips_kernel,
        out_shape=(
            jax.ShapeDtypeStruct((3, 2 * SIDE, SIDE, SIDE, 32, LANES), f32),
            jax.ShapeDtypeStruct((2, LANES), jnp.int32),
        ),
        in_specs=[smem] * 3 + [anywhere] * 6,
        out_specs=[anywhere, vmem],
        scratch_shapes=[
            pltpu.VMEM((3, 2 * SIDE, SIDE, SIDE, 32, LANES), f32),
            pltpu.VMEM(inverse.shape, f32),
            pltpu.VMEM((SIDE, archs * modes * 3 // 2, LANES), f32),
            pltpu.VMEM((SIDE, archs * LANES, LANES), f32),
            pltpu.VMEM(offset.shape, f32),
            pltpu.VMEM((instances, LANES, LANES), f32),
            pltpu.VMEM((count, modes, LANES), f32),
            pltpu.VMEM((count, modes, LANES), f32),
            pltpu.VMEM((count, LANES, LANES), f32),
            pltpu.VMEM((count * 4, 32, LANES), f32),
            pltpu.VMEM((instances * 4, 32, LANES), f32),
            pltpu.VMEM((instances, LANES), f32),
            pltpu.VMEM(params.shape, f32),
            pltpu.SMEM(rows.shape, jnp.int32),
            pltpu.VMEM((16, LANES), jnp.int32),
            pltpu.SMEM((16, LANES), jnp.int32),
            pltpu.VMEM((3, SIDE, SIDE, 8, 32, LANES), f32),
            pltpu.VMEM((3, SIDE, SIDE, 8, 32, LANES), f32),
            pltpu.VMEM((3, SIDE, SIDE, 8, 32, LANES), f32),
            dma((7,)),
            dma((2, 3, 2)),
            dma((2, 3, 2)),
            dma((2, 3, 2, 3)),
            dma((2, 3, 2, 3)),
            dma((2, 3, 2)),
            dma((2, 3, 2)),
            dma((3, 2, 4)),
            dma((3, 8)),
            dma((3, 3)),
            dma((3, 3, 4)),
            dma((3, 7, 4)),
            dma((3, 3, 7)),
        ],
        compiler_params=pltpu.CompilerParams(
            collective_id=0, has_side_effects=True, vmem_limit_bytes=VMEM_LIMIT
        ),
        name="strips",
    )(arch, param, ports, rows, params, inverse, coupling, stiffness, offset)


AHEAD = 16


def assemble_kernel(where, arrived, out, even, odd, rows, in_sems, out_sems):
    groups = rows.shape[0]

    def fetch(group):
        for r in range(8):
            for parity, buffer in enumerate((even, odd)):
                pltpu.make_async_copy(
                    arrived.at[where[(group * 8 + r) * 2 + parity]],
                    buffer.at[group, :, r],
                    in_sems.at[group, parity],
                ).start()

    def written(group):
        begin = pl.multiple_of(group * 8, 8)
        return pltpu.make_async_copy(rows.at[group], out.at[pl.ds(begin, 8)], out_sems.at[group])

    lane = lax.broadcasted_iota(jnp.int32, (8, LANES), 1)
    for group in range(AHEAD):
        fetch(group)

    def lay_out(group, carry):
        @pl.when(group + AHEAD < groups)
        def _():
            fetch(group + AHEAD)

        take(even.at[group], in_sems.at[group, 0])
        take(odd.at[group], in_sems.at[group, 1])

        def row(i):
            e, o = even[group, i], odd[group, i]
            return jnp.where(lane < 32, e + o, e), o

        for g in range(8):
            (s0, o0), (s1, o1), (s2, o2), (s3, o3) = (row(4 * g + i) for i in range(4))
            if g == 0:
                s1 = jnp.where(lane == 0, pltpu.roll(s0, LANES - 1, 1), s1)
            tiles = (
                s0,
                pltpu.roll(jnp.where(lane < 32, s1, o0), 96, 1),
                jnp.where(lane < 96, pltpu.roll(s1, 96, 1), pltpu.roll(o1, 64, 1)),
                pltpu.roll(jnp.where(lane < 64, s2, o1), 64, 1),
                jnp.where(lane < 64, pltpu.roll(s2, 64, 1), pltpu.roll(o2, 32, 1)),
                pltpu.roll(jnp.where(lane < 96, s3, o2), 32, 1),
                jnp.where(lane < 32, pltpu.roll(s3, 32, 1), o3),
            )
            for t, tile in enumerate(tiles):
                rows[group, :, (7 * g + t) * LANES : (7 * g + t + 1) * LANES] = tile
        written(group).start()
        return carry

    lax.fori_loop(0, groups, lay_out, 0)

    def finish(group, carry):
        written(group).wait()
        return carry

    lax.fori_loop(0, groups, finish, 0)


def assemble(where, arrived, ports):
    groups = ports // 8
    return pl.pallas_call(
        assemble_kernel,
        out_shape=jax.ShapeDtypeStruct((ports, 56 * LANES), jnp.float32),
        in_specs=[pl.BlockSpec(memory_space=pltpu.SMEM), pl.BlockSpec(memory_space=pl.ANY)],
        out_specs=pl.BlockSpec(memory_space=pl.ANY),
        scratch_shapes=[
            pltpu.VMEM((groups, 32, 8, LANES), jnp.float32),
            pltpu.VMEM((groups, 32, 8, LANES), jnp.float32),
            pltpu.VMEM((groups, 8, 56 * LANES), jnp.float32),
            pltpu.SemaphoreType.DMA((groups, 2)),
            pltpu.SemaphoreType.DMA((groups,)),
        ],
        compiler_params=pltpu.CompilerParams(vmem_limit_bytes=VMEM_LIMIT),
        name="assemble",
    )(where, arrived)


def body(
    instance_arch,
    instance_param,
    instance_ports,
    port_row,
    param_table,
    bubble_inverse,
    coupling,
    port_stiffness,
    coupling_offset,
):
    instances = instance_arch.shape[0]
    ports = 2 * instances
    archs, modes = coupling.shape[:2]
    arrived, where = strips_of(
        instance_arch,
        instance_param,
        instance_ports.T,
        port_row,
        param_table.T,
        bubble_inverse,
        coupling.reshape(archs * modes, LANES),
        port_stiffness.reshape(archs * LANES, LANES),
        coupling_offset,
    )
    return assemble(where.reshape(2 * ports), arrived.reshape(384, 32, LANES), ports)


def solution(mesh):
    return jax.shard_map(
        body,
        mesh=mesh,
        in_specs=(
            P(("inst", "arch")),
            P(("inst", "arch")),
            P(("inst", "arch"), None),
            P(),
            P(),
            P("arch", None, None),
            P("arch", None, None),
            P("arch", None, None),
            P(("inst", "arch"), None, None),
        ),
        out_specs=P(("inst", "arch"), None),
        check_vma=False,
    )
```

```python
import functools

import jax
import jax.numpy as jnp
from jax import lax
from jax.experimental import pallas as pl
from jax.experimental.pallas import tpu as pltpu
from jax.sharding import PartitionSpec as P

MESH = pl.DeviceIdType.MESH
SIDE = 4
OFFSETS = (1, 3, 2)
LANES = 128
VMEM_LIMIT = 56 << 20
UNROLL = 16


def position():
    inst, z = lax.axis_index("inst"), lax.axis_index("arch")
    return inst // (2 * SIDE), inst // 2 % SIDE, inst % 2, z


def device(x, y, core, z):
    return ((x * SIDE + y) * 2 + core, z)


def moved(here, axis, offset):
    there = list(here)
    there[axis] = (there[axis] + offset) % SIDE
    return tuple(there)


def greet(partners):
    barrier = pltpu.get_barrier_semaphore()
    for partner in partners:
        pl.semaphore_signal(barrier, inc=1, device_id=device(*partner), device_id_type=MESH)
    pl.semaphore_wait(barrier, len(partners))


def send(src, dst, send_sem, recv_sem, there):
    copy = pltpu.make_async_remote_copy(
        src, dst, send_sem, recv_sem, device_id=device(*there), device_id_type=MESH
    )
    copy.start()
    return copy


def take(ref, sem):
    pltpu.make_async_copy(ref, ref, sem).wait()


PIECES = ((64, 56), (80, 80))
ORDERS = ((0, 1, 3), (1, 3, 0), (3, 0, 1))


def halves(value):
    high = value.astype(jnp.bfloat16).astype(jnp.float32)
    return high, value - high


def reorder(v, k):
    if k == 0:
        return v
    lane = lax.broadcasted_iota(jnp.int32, v.shape, 1)
    first = pltpu.roll(v, LANES - 32 * k, 1)
    after = pltpu.roll(v, 32, 1)
    return jnp.where(lane < 32, first, jnp.where(lane < 32 * (k + 1), after, v))


def strips_kernel(
    arch,
    param,
    ports,
    row_in,
    params_in,
    inverse_in,
    coupling_in,
    stiffness_in,
    offset_in,
    arrived_out,
    where,
    arrived,
    inverse,
    basis,
    stiff,
    offset,
    turned,
    inverse_table,
    natural,
    coupling_table,
    stiff_table,
    strips,
    scales,
    params,
    rows,
    slots_vector,
    slots,
    first,
    second,
    third,
    local,
    s1,
    r1,
    s2,
    r2,
    s3,
    r3,
    here_sems,
    out_sems,
    ss1,
    ss2,
    ss3,
    rs,
):
    here = position()
    x, y, core, z = here
    other = (x, y, 1 - core, z)
    lines = {axis: [moved(here, axis, o) for o in OFFSETS] for axis in (0, 1, 3)}
    archs, modes = inverse.shape[0], inverse.shape[1]
    instances = offset.shape[0]
    half_modes = modes // 2
    inverse_rows, coupling_rows = archs * half_modes, archs * modes
    own = [
        pltpu.make_async_copy(inverse_in, inverse, local.at[0]),
        pltpu.make_async_copy(coupling_in, basis.at[z, pl.ds(inverse_rows, coupling_rows)], local.at[1]),
        pltpu.make_async_copy(stiffness_in, stiff.at[z], local.at[2]),
        pltpu.make_async_copy(offset_in, offset, local.at[3]),
        pltpu.make_async_copy(row_in, rows, local.at[4]),
        pltpu.make_async_copy(params_in, params, local.at[5]),
    ]
    for copy in own:
        copy.start()
    partners = [other]
    for axis in (0, 1, 3):
        for there in lines[axis]:
            partners += [there, (there[0], there[1], 1 - core, there[3])]
    greet(partners)

    lane = lax.broadcasted_iota(jnp.int32, (LANES, LANES), 1)
    left = lane < modes
    left_half = left[:half_modes]
    row8 = lax.broadcasted_iota(jnp.int32, (8, LANES), 0)
    lane8 = lane[:8]

    own[0].wait()
    for a in range(archs):
        top = jnp.concatenate([inverse[a, :half_modes], inverse[a, half_modes:]], axis=1)
        basis[z, a * half_modes : (a + 1) * half_modes] = top
    own[1].wait()
    arrays = ((basis, PIECES[0]), (stiff, PIECES[1]))

    def piece(a, half, plane):
        ref, sizes = arrays[a]
        size, base = sizes[half], half * 8 * sizes[0]
        return ref.at[plane, pl.ds(base + (core * SIDE + here[half]) * size, size)]

    def core_half(a, half, plane, which):
        ref, sizes = arrays[a]
        size, base = sizes[half], half * 8 * sizes[0]
        return ref.at[plane, pl.ds(base + which * SIDE * size, SIDE * size)]

    sent = []
    planes = [(z + SIDE - o) % SIDE for o in OFFSETS]

    def along_z(a):
        for o, there in enumerate(lines[3]):
            for half in (0, 1):
                mine = piece(a, half, z)
                sent.append(send(mine, mine, s1.at[a, o, half], r1.at[a, o, half], there))

    def along_lines(a):
        for o, plane in enumerate(planes):
            for half in (0, 1):
                got = piece(a, half, plane)
                take(got, r1.at[a, o, half])
                for i, there in enumerate(lines[half]):
                    sent.append(send(got, got, s2.at[a, o, half, i], r2.at[a, o, half, i], there))

    def to_other_core(a):
        for o, plane in enumerate(planes):
            for half in (0, 1):
                for i in range(3):
                    take(piece(a, half, plane), r2.at[a, o, half, i])
                got = core_half(a, half, plane, core)
                sent.append(send(got, got, s3.at[a, o, half], r3.at[a, o, half], other))

    def wait_plane(a, o):
        for half in (0, 1):
            take(core_half(a, half, planes[o], 1 - core), r3.at[a, o, half])

    def doubled(one, other):
        both = jnp.concatenate([one, other], axis=0).T
        flipped = pltpu.roll(both, modes, 1)
        return jnp.where(left, both, flipped), jnp.where(left, flipped, both)

    def basis_tables(plane):
        def one(at, carry):
            packed = basis[plane, pl.ds(pl.multiple_of(at * half_modes, half_modes), half_modes), :]
            flipped = pltpu.roll(packed, modes, 1)
            both = jnp.concatenate(
                [jnp.where(left_half, packed, flipped), jnp.where(left_half, flipped, packed)], axis=0
            )
            inverse_table[plane * archs + at] = both
            return carry

        lax.fori_loop(0, archs, one, 0, unroll=5)

        def two(pair, carry):
            begin = pl.multiple_of(inverse_rows + pair * 2 * modes, half_modes)
            c = basis[plane, pl.ds(begin, modes), :]
            d = basis[plane, pl.ds(pl.multiple_of(begin + modes, half_modes), modes), :]
            at = plane * archs + pair * 2
            natural[at], natural[at + 1] = c, d
            coupling_table[at], coupling_table[at + 1] = doubled(c, d)
            return carry

        lax.fori_loop(0, archs // 2, two, 0, unroll=5)

    def stiff_tables(plane):
        def one(at, carry):
            for k in range(4):
                begin = pl.multiple_of(at * LANES + k * 32, 32)
                stiff_table[(plane * archs + at) * 4 + k] = reorder(stiff[plane, pl.ds(begin, 32), :], k)
            return carry

        lax.fori_loop(0, archs, one, 0, unroll=5)

    def turn(begin, end):
        def one(i, carry):
            first_of_two, second_of_two = doubled(offset[2 * i], offset[2 * i + 1])
            turned[2 * i] = first_of_two
            turned[2 * i + 1] = second_of_two
            return carry

        lax.fori_loop(begin // 2, end // 2, one, 0, unroll=4)

    def look_up_scales():
        wanted = jnp.zeros((8, LANES), jnp.int32)
        for i in range(instances):
            wanted = jnp.where(lane8 == i, param[i], wanted)
        samples = params.shape[1]
        sample = lax.broadcasted_iota(jnp.int32, (samples, LANES), 0)
        chosen = jnp.where(sample == wanted[:1], 1.0, 0.0).astype(jnp.bfloat16)
        high, rest = halves(params[...])
        middle, low = halves(rest)
        found = jnp.zeros((modes, LANES), jnp.float32)
        for part in (high, middle, low):
            found = found + jnp.dot(part.astype(jnp.bfloat16), chosen, preferred_element_type=jnp.float32)
        scales[...] = jnp.concatenate([found, found], axis=0).T[:instances]

    def place_strips():
        def one(i, carry):
            low, high = carry
            low = jnp.where(lane8 == i, rows[ports[0, i]], low)
            low = jnp.where(lane8 == i + instances, rows[ports[1, i]], low)
            high = jnp.where(lane8 == i, rows[ports[2, i]], high)
            high = jnp.where(lane8 == i + instances, rows[ports[3, i]], high)
            return low, high

        zero = jnp.zeros((8, LANES), jnp.int32)
        row = lax.fori_loop(0, instances, one, (zero, zero), unroll=8)

        def down(v):
            return jnp.broadcast_to(v[:1], (LANES, LANES)).T

        wanted = jnp.zeros((8, LANES), jnp.int32)
        for i in range(instances):
            wanted = jnp.where((lane8 == i) | (lane8 == i + instances), arch[i] * 4, wanted)
        sub = lax.broadcasted_iota(jnp.int32, (LANES, LANES), 0)
        owner = [v >> 7 for v in row]
        owner_down = [down(v) for v in owner]
        places, values = [], []
        for h in (0, 1):
            across = owner[h][:1]
            same = jnp.where((owner_down[h] == across) & (sub < lane), 1, 0)
            if h == 1:
                same = same + jnp.where(owner_down[0] == across, 1, 0)
            ordinal = jnp.sum(same, axis=0, keepdims=True)
            oz, oc, oy, ox = across & 3, (across >> 2) & 1, (across >> 3) & 3, across >> 5
            place = jnp.where(
                ordinal == 0,
                (ox * 4 + oy) * 8 + oz * 2 + oc,
                jnp.where(
                    ordinal == 1,
                    128 + (oy * 4 + oz) * 8 + ox * 2 + oc,
                    256 + (oz * 4 + ox) * 8 + oy * 2 + oc,
                ),
            )
            odd = jnp.where(lane8[:1] < instances, 0, 1)
            code = (row[h][:1] & 127) * 2 + odd
            stiff_at = wanted[:1] + odd + 2 * h
            places.append(down(place))
            values.append(down((stiff_at << 17) + ((code + 1) << 8) + lane8[:1] + h * LANES))
        for j in range(3):
            target = lane8[:1] + j * LANES
            total = jnp.zeros((LANES, LANES), jnp.int32)
            for h in (0, 1):
                total = jnp.maximum(total, jnp.where(places[h] == target, values[h], 0))
            value = jnp.max(total, axis=0, keepdims=True)
            slots_vector[j : j + 1] = value & 255
            slots_vector[j + 3 : j + 4] = ((value >> 8) & 511) - 1
            slots_vector[j + 6 : j + 7] = value >> 17

    along_z(0)
    own[2].wait()
    along_z(1)
    own[4].wait()
    place_strips()
    to_scalars = pltpu.make_async_copy(slots_vector, slots, local.at[6])
    to_scalars.start()
    along_lines(0)
    own[3].wait()
    own[5].wait()
    turn(0, instances)
    basis_tables(z)
    look_up_scales()
    to_other_core(0)
    along_lines(1)
    for o in range(3):
        wait_plane(0, o)
        basis_tables(planes[o])
    to_other_core(1)

    left_modes = left[:modes]

    def condense(step, carry):
        applied = []
        for u in range(UNROLL):
            i = step * UNROLL + u
            a = arch[i]
            scaled = inverse_table[a] * scales[pl.ds(i, 1), :]
            mixed = jnp.where(left_modes, scaled, halves(scaled)[1]).astype(jnp.bfloat16)
            high, low = halves(natural[a] + offset[i])
            applied.append(
                jnp.dot(
                    jnp.concatenate([mixed, mixed], axis=1),
                    jnp.concatenate([high, high, low, low], axis=0).astype(jnp.bfloat16),
                    preferred_element_type=jnp.float32,
                )
            )
        for u in range(UNROLL):
            i = step * UNROLL + u
            high, low = halves(applied[u])
            weighted = (coupling_table[arch[i]] + turned[i]) * scales[pl.ds(i, 1), :]
            mixed = jnp.where(left, weighted, halves(weighted)[1]).astype(jnp.bfloat16)
            product = jnp.dot(
                jnp.concatenate([mixed, mixed], axis=1),
                jnp.concatenate([high, high, low, low], axis=0).astype(jnp.bfloat16),
                preferred_element_type=jnp.float32,
            )
            for k in range(4):
                strips[k * instances + i] = reorder(product[k * 32 : (k + 1) * 32], k)
        return carry

    lax.fori_loop(0, instances // UNROLL, condense, 0)
    stiff_tables(z)
    for o in range(3):
        wait_plane(1, o)
        stiff_tables(planes[o])

    to_scalars.wait()
    spot = (row8 == 1) & (lane8 == 0)

    def pack(part, line, into):
        def one(i, carry):
            at = line * 32 + i
            strip = slots[part, at]
            stiff_at = slots[part + 6, at]
            into[i // 8, i % 8, 8:] = stiff_table[stiff_at, 8:] - strips[strip, 8:]
            top = stiff_table[stiff_at, :8] - strips[strip, :8]
            into[i // 8, i % 8, :8] = jnp.where(spot, slots[part + 3, at].astype(jnp.float32), top)
            return carry

        lax.fori_loop(0, 32, one, 0, unroll=8)

    for i, o in enumerate(OFFSETS):
        for part, (a1, a2, a3) in enumerate(ORDERS):
            line = (here[a1] + o) % SIDE
            pack(part, line, first.at[part, line])
            there = moved(here, a1, o)
            sent.append(
                send(
                    first.at[part, line],
                    second.at[part, here[a1]],
                    ss1.at[part, i],
                    rs.at[part, 0, i],
                    there,
                )
            )
    for part, (a1, a2, a3) in enumerate(ORDERS):
        pack(part, here[a1], second.at[part, here[a1]])
    kept = [[], [], []]
    for n, o in enumerate((0, *OFFSETS)):
        for part, (a1, a2, a3) in enumerate(ORDERS):
            source = (here[a1] + SIDE - o) % SIDE
            if o:
                take(second.at[part, source], rs.at[part, 0, n - 1])
            dst = third.at[part, here[a2], source]
            for i, p in enumerate(OFFSETS):
                there = moved(here, a2, p)
                src = second.at[part, source, there[a2]]
                sent.append(send(src, dst, ss2.at[part, i, n], rs.at[part, 1, i], there))
            copy = pltpu.make_async_copy(
                second.at[part, source, here[a2]], dst, here_sems.at[part, 0, n]
            )
            copy.start()
            kept[part].append(copy)
    own_strips = [[], [], []]
    for n, o in enumerate((0, *OFFSETS)):
        for part, (a1, a2, a3) in enumerate(ORDERS):
            source = (here[a2] + SIDE - o) % SIDE
            if o:
                take(third.at[part, source], rs.at[part, 1, n - 1])
            else:
                for copy in kept[part]:
                    copy.wait()
            dst = arrived.at[part, here[a3] * 2 + core, source]
            i = 0
            for p in (*OFFSETS, 0):
                for flip in (0, 1):
                    there = moved(here, a3, p)
                    to = (core + flip) % 2
                    there = (there[0], there[1], to, there[3])
                    src = third.at[part, source, :, there[a3] * 2 + to]
                    if p == 0 and flip == 0:
                        copy = pltpu.make_async_copy(src, dst, here_sems.at[part, 1, n])
                        copy.start()
                        own_strips[part].append(copy)
                    else:
                        sent.append(send(src, dst, ss3.at[part, i, n], rs.at[part, 2, i], there))
                        i += 1
    landed = arrived.reshape(384 * 32, LANES)
    found = [jnp.zeros((8, LANES), jnp.int32)] * 2
    out = []
    for n, (o, flip) in enumerate([(o, flip) for o in (0, *OFFSETS) for flip in (0, 1)]):
        for part, (a1, a2, a3) in enumerate(ORDERS):
            origin = (here[a3] + SIDE - o) % SIDE * 2 + (core + flip) % 2
            if n == 0:
                for copy in own_strips[part]:
                    copy.wait()
            else:
                take(arrived.at[part, origin], rs.at[part, 2, (n + 5) % 7])
            copy = pltpu.make_async_copy(
                arrived.at[part, origin], arrived_out.at[part, origin], out_sems.at[part, n]
            )
            copy.start()
            out.append(copy)
            strip = (part * 2 * SIDE + origin) * SIDE * SIDE
            for g in (0, 8):
                codes = landed[pl.ds((strip + g) * 32 + 1, 8, stride=32), :][:, :1]
                for t in (0, 1):
                    hit = codes == (lane8 + t * LANES).astype(jnp.float32)
                    found[t] = found[t] + jnp.where(hit, row8 + (strip + g), 0)
    for t in (0, 1):
        where[t : t + 1, :] = jnp.sum(found[t], axis=0, keepdims=True)
    for copy in sent:
        copy.wait_send()
    for copy in out:
        copy.wait()


def strips_of(arch, param, ports, rows, params, inverse, coupling, stiffness, offset):
    dma = pltpu.SemaphoreType.DMA
    archs, modes = inverse.shape[:2]
    instances, count = offset.shape[0], SIDE * archs
    f32 = jnp.float32
    assert archs % 2 == 0 and archs * modes * 3 // 2 == 8 * sum(PIECES[0]) and archs * LANES == 8 * sum(PIECES[1])
    smem, vmem, anywhere = (
        pl.BlockSpec(memory_space=m) for m in (pltpu.SMEM, pltpu.VMEM, pl.ANY)
    )
    return pl.pallas_call(
        strips_kernel,
        out_shape=(
            jax.ShapeDtypeStruct((3, 2 * SIDE, SIDE, SIDE, 32, LANES), f32),
            jax.ShapeDtypeStruct((2, LANES), jnp.int32),
        ),
        in_specs=[smem] * 3 + [anywhere] * 6,
        out_specs=[anywhere, vmem],
        scratch_shapes=[
            pltpu.VMEM((3, 2 * SIDE, SIDE, SIDE, 32, LANES), f32),
            pltpu.VMEM(inverse.shape, f32),
            pltpu.VMEM((SIDE, archs * modes * 3 // 2, LANES), f32),
            pltpu.VMEM((SIDE, archs * LANES, LANES), f32),
            pltpu.VMEM(offset.shape, f32),
            pltpu.VMEM((instances, LANES, LANES), f32),
            pltpu.VMEM((count, modes, LANES), f32),
            pltpu.VMEM((count, modes, LANES), f32),
            pltpu.VMEM((count, LANES, LANES), f32),
            pltpu.VMEM((count * 4, 32, LANES), f32),
            pltpu.VMEM((instances * 4, 32, LANES), f32),
            pltpu.VMEM((instances, LANES), f32),
            pltpu.VMEM(params.shape, f32),
            pltpu.SMEM(rows.shape, jnp.int32),
            pltpu.VMEM((16, LANES), jnp.int32),
            pltpu.SMEM((16, LANES), jnp.int32),
            pltpu.VMEM((3, SIDE, SIDE, 8, 32, LANES), f32),
            pltpu.VMEM((3, SIDE, SIDE, 8, 32, LANES), f32),
            pltpu.VMEM((3, SIDE, SIDE, 8, 32, LANES), f32),
            dma((7,)),
            dma((2, 3, 2)),
            dma((2, 3, 2)),
            dma((2, 3, 2, 3)),
            dma((2, 3, 2, 3)),
            dma((2, 3, 2)),
            dma((2, 3, 2)),
            dma((3, 2, 4)),
            dma((3, 8)),
            dma((3, 3)),
            dma((3, 3, 4)),
            dma((3, 7, 4)),
            dma((3, 3, 7)),
        ],
        compiler_params=pltpu.CompilerParams(
            collective_id=0, has_side_effects=True, vmem_limit_bytes=VMEM_LIMIT
        ),
        name="strips",
    )(arch, param, ports, rows, params, inverse, coupling, stiffness, offset)


AHEAD = 16


def assemble_kernel(where, arrived, out, even, odd, rows, in_sems, out_sems):
    groups = rows.shape[0]

    def fetch(group):
        for r in range(8):
            for parity, buffer in enumerate((even, odd)):
                pltpu.make_async_copy(
                    arrived.at[where[(group * 8 + r) * 2 + parity]],
                    buffer.at[group, :, r],
                    in_sems.at[group, parity],
                ).start()

    def written(group):
        begin = pl.multiple_of(group * 8, 8)
        return pltpu.make_async_copy(rows.at[group], out.at[pl.ds(begin, 8)], out_sems.at[group])

    lane = lax.broadcasted_iota(jnp.int32, (8, LANES), 1)
    for group in range(AHEAD):
        fetch(group)

    def lay_out(group, carry):
        @pl.when(group + AHEAD < groups)
        def _():
            fetch(group + AHEAD)

        take(even.at[group], in_sems.at[group, 0])
        take(odd.at[group], in_sems.at[group, 1])

        def row(i):
            e, o = even[group, i], odd[group, i]
            return jnp.where(lane < 32, e + o, e), o

        for g in range(8):
            (s0, o0), (s1, o1), (s2, o2), (s3, o3) = (row(4 * g + i) for i in range(4))
            if g == 0:
                s1 = jnp.where(lane == 0, pltpu.roll(s0, LANES - 1, 1), s1)
            tiles = (
                s0,
                pltpu.roll(jnp.where(lane < 32, s1, o0), 96, 1),
                jnp.where(lane < 96, pltpu.roll(s1, 96, 1), pltpu.roll(o1, 64, 1)),
                pltpu.roll(jnp.where(lane < 64, s2, o1), 64, 1),
                jnp.where(lane < 64, pltpu.roll(s2, 64, 1), pltpu.roll(o2, 32, 1)),
                pltpu.roll(jnp.where(lane < 96, s3, o2), 32, 1),
                jnp.where(lane < 32, pltpu.roll(s3, 32, 1), o3),
            )
            for t, tile in enumerate(tiles):
                rows[group, :, (7 * g + t) * LANES : (7 * g + t + 1) * LANES] = tile
        written(group).start()
        return carry

    lax.fori_loop(0, groups, lay_out, 0)

    def finish(group, carry):
        written(group).wait()
        return carry

    lax.fori_loop(0, groups, finish, 0)


def assemble(where, arrived, ports):
    groups = ports // 8
    return pl.pallas_call(
        assemble_kernel,
        out_shape=jax.ShapeDtypeStruct((ports, 56 * LANES), jnp.float32),
        in_specs=[pl.BlockSpec(memory_space=pltpu.SMEM), pl.BlockSpec(memory_space=pl.ANY)],
        out_specs=pl.BlockSpec(memory_space=pl.ANY),
        scratch_shapes=[
            pltpu.VMEM((groups, 32, 8, LANES), jnp.float32),
            pltpu.VMEM((groups, 32, 8, LANES), jnp.float32),
            pltpu.VMEM((groups, 8, 56 * LANES), jnp.float32),
            pltpu.SemaphoreType.DMA((groups, 2)),
            pltpu.SemaphoreType.DMA((groups,)),
        ],
        compiler_params=pltpu.CompilerParams(vmem_limit_bytes=VMEM_LIMIT),
        name="assemble",
    )(where, arrived)


def body(
    instance_arch,
    instance_param,
    instance_ports,
    port_row,
    param_table,
    bubble_inverse,
    coupling,
    port_stiffness,
    coupling_offset,
):
    instances = instance_arch.shape[0]
    ports = 2 * instances
    archs, modes = coupling.shape[:2]
    arrived, where = strips_of(
        instance_arch,
        instance_param,
        instance_ports.T,
        port_row,
        param_table.T,
        bubble_inverse,
        coupling.reshape(archs * modes, LANES),
        port_stiffness.reshape(archs * LANES, LANES),
        coupling_offset,
    )
    return assemble(where.reshape(2 * ports), arrived.reshape(384, 32, LANES), ports)


def solution(mesh):
    return jax.shard_map(
        body,
        mesh=mesh,
        in_specs=(
            P(("inst", "arch")),
            P(("inst", "arch")),
            P(("inst", "arch"), None),
            P(),
            P(),
            P("arch", None, None),
            P("arch", None, None),
            P("arch", None, None),
            P(("inst", "arch"), None, None),
        ),
        out_specs=P(("inst", "arch"), None),
        check_vma=False,
    )
```
